32 devices in a mesh: lon: 8 (over z, y), lev: 4 (over x, core).
Axes of the slice: x: 2, y: 2, z: 4, core: 2. Of those that a mesh axis runs over, the one named last changes fastest.
Arguments:
- column_old: float32 [70, 262144], P(None, ('lon', 'lev')), may hold values from -6 to 6
- coupling: float32 [69, 262144], P(None, ('lon', 'lev')), may hold values from 7.5 to 120, as said below
- sea_temp: float32 [262144], P(('lon', 'lev')), may hold values from -6 to 6
- land_mask: int32 [262144], P(('lon', 'lev')), may hold values from 0 to 1, as said below
- tile_weight: float32 [9, 262144], P(None, ('lon', 'lev')), may hold values from 0.05 to 1
- tile_coeff: float32 [9, 262144], P(None, ('lon', 'lev')), may hold values from 0.2 to 5
- tile_capacity: float32 [9, 262144], P(None, ('lon', 'lev')), may hold values from 0.5 to 5
- tile_conduct: float32 [9, 262144], P(None, ('lon', 'lev')), may hold values from 0.1 to 2
- tile_old: float32 [9, 262144], P(None, ('lon', 'lev')), may hold values from -6 to 6
- tile_forcing: float32 [9, 262144], P(None, ('lon', 'lev')), may hold values from -12 to 12
Outputs:
- column_temp: float32 [70, 262144], P(None, ('lon', 'lev'))
- tile_temp: float32 [9, 262144], P(None, ('lon', 'lev'))
The draws below stay inside these ranges and needn't reach their ends.
Inputs may be any that keep to these rules, and one draw needn't show every extreme that they name: `land_mask`: 1 marks a land column, 0 an ocean column. `coupling`: positive.
All inputs are finite; a program needn't handle non-finite values.
Results may differ from the reference program's by a relative error of at most 0.0001.
Values sent between devices are 32-bit elements; how exact they have to be, the bound alone decides.
No kernel may reach another device: no remote copies, remote signals or barrier semaphores. Data moves between devices by JAX's collectives and lax.ppermute only.
A program may use at most 64 MiB of HBM per device.

```python
import math
import jax
import jax.numpy as jnp
from jax import lax

COLS_DEV = 8192
LEV = 70
NT = 9
ITERS = 8
COLUMNS = 262144
N_LON = 8
N_LEV = 4


def draw_land_mask(key, part):
    first_key = jax.random.fold_in(key, 11)
    second_key = jax.random.fold_in(key, 12)
    blocks = COLUMNS // COLS_DEV
    land_level = jax.random.randint(first_key, (blocks, 1), 0, 9)
    column_roll = jax.random.randint(second_key, (blocks, COLS_DEV), 0, 8)
    return (column_roll < land_level).astype(jnp.int32).reshape(COLUMNS)


def draw_coupling(key, part):
    base_key = jax.random.fold_in(key, 21)
    rough_key = jax.random.fold_in(key, 22)
    tiles = COLUMNS // 128
    base_log = jax.random.uniform(base_key, (1, tiles), jnp.float32, math.log(15.0), math.log(60.0))
    base = jnp.repeat(jnp.exp(base_log), 128, axis=1)
    rough_log = jax.random.uniform(rough_key, (LEV - 1, COLUMNS), jnp.float32, math.log(0.5), math.log(2.0))
    rough = jnp.exp(rough_log)
    return (base * rough).astype(jnp.float32)


def block_levels(own_key, dims, shards, smallest, high):
    factor_of, own = 1.0, jax.random.fold_in(own_key, 6)
    for position, blocks in shards:
        draws = jnp.exp(jax.random.uniform(jax.random.fold_in(own, position), (blocks,), jnp.float32, smallest / len(shards), high / len(shards)))
        factor_of = factor_of * jnp.repeat(draws, dims[position] // blocks).reshape([-1 if axis == position else 1 for axis in range(len(dims))])
    return factor_of


def normal_values(key, shape, scale, bound, split=(), held_as=jnp.bfloat16):
    factor_of = block_levels(key, shape, split, -0.22, 0.18) if split else 1.0
    array = jax.random.normal(key, shape, jnp.float32) * scale * factor_of
    return jnp.minimum(jnp.maximum(array, -bound), bound).astype(held_as)


def setup_inputs(seed: int = 0) -> dict:
    key_of = jax.random.split(jax.random.key(seed), 11)
    column_old = normal_values(key_of[0], (LEV, COLUMNS), 1.0, 6.0, ((1, 32),), jnp.float32)
    coupling = draw_coupling(jax.random.fold_in(key_of[10], 71), 0)
    sea_temp = normal_values(key_of[2], (COLUMNS,), 1.0, 6.0, ((0, 32),), jnp.float32)
    land_mask = draw_land_mask(jax.random.fold_in(key_of[10], 71), 0)
    tile_weight = jnp.clip(jnp.exp(math.log(1.0) - 2.9957323 * jax.random.uniform(key_of[4], (NT, COLUMNS), jnp.float32) ** block_levels(key_of[4], (NT, COLUMNS), ((1, 32),), -0.2, 0.2)), 0.05, 1.0)
    tile_coeff = jnp.clip(jnp.exp(math.log(5.0) - 3.218876 * jax.random.uniform(key_of[5], (NT, COLUMNS), jnp.float32) ** block_levels(key_of[5], (NT, COLUMNS), ((1, 32),), -0.2, 0.2)), 0.2, 5.0)
    tile_capacity = jnp.clip(jnp.exp(math.log(5.0) - 2.3025851 * jax.random.uniform(key_of[6], (NT, COLUMNS), jnp.float32) ** block_levels(key_of[6], (NT, COLUMNS), ((1, 32),), -0.2, 0.2)), 0.5, 5.0)
    tile_conduct = jnp.clip(jnp.exp(math.log(2.0) - 2.9957323 * jax.random.uniform(key_of[7], (NT, COLUMNS), jnp.float32) ** block_levels(key_of[7], (NT, COLUMNS), ((1, 32),), -0.2, 0.2)), 0.1, 2.0)
    tile_old = normal_values(key_of[8], (NT, COLUMNS), 1.0, 6.0, ((1, 32),), jnp.float32)
    tile_forcing = normal_values(key_of[9], (NT, COLUMNS), 2.0, 12.0, ((1, 32),), jnp.float32)
    return {"column_old": column_old, "coupling": coupling, "sea_temp": sea_temp, "land_mask": land_mask, "tile_weight": tile_weight, "tile_coeff": tile_coeff, "tile_capacity": tile_capacity, "tile_conduct": tile_conduct, "tile_old": tile_old, "tile_forcing": tile_forcing}


def eliminate_upper(column_old, smooth):
    zero_row = jnp.zeros_like(smooth[:1])
    k_below = smooth[1:]
    k_above = jnp.concatenate([smooth[2:], zero_row], axis=0)

    def one_level(carried, layer_data):
        offset_next, factor_next = carried
        right_side, below_k, above_k = layer_data
        pivots = 1.0 + below_k + above_k - above_k * factor_next
        offset = (right_side + above_k * offset_next) / pivots
        factor = below_k / pivots
        return (offset, factor), (offset, factor)

    initial = (jnp.zeros_like(column_old[0]), jnp.zeros_like(column_old[0]))
    last, stacked = lax.scan(one_level, initial, (column_old[2:], k_below, k_above), reverse=True, unroll=4)
    return last[0], last[1], stacked[0], stacked[1]


def lower_levels(column_old, smooth, offset_two, factor_two, surface_flux):
    k_ground = smooth[0] * (1.0 + 0.5 * jnp.tanh(surface_flux))
    k_second = smooth[1]
    pivot_one = 1.0 + k_ground + k_second - k_second * factor_two
    offset_one = (column_old[1] + k_second * offset_two) / pivot_one
    factor_one = k_ground / pivot_one
    pivot_ground = 1.0 + k_ground - k_ground * factor_one
    return (column_old[0] + k_ground * offset_one) / pivot_ground, 1.0 / pivot_ground, offset_one, factor_one


def surface_solve(p_surf, q_surf, column_a, column_b):
    return (p_surf + q_surf * column_a) / (1.0 + q_surf * column_b)


def tile_sums(tile_weight, tile_coeff, tile_capacity, tile_conduct, tile_old, tile_forcing):
    fraction = tile_weight / jnp.sum(tile_weight, axis=0)
    denominator = tile_capacity + tile_coeff + tile_conduct
    source = tile_capacity * tile_old + tile_forcing
    land_a = jnp.sum(fraction * tile_coeff * source / denominator, axis=0)
    land_b = jnp.sum(fraction * tile_coeff * (tile_capacity + tile_conduct) / denominator, axis=0)
    return land_a, land_b, denominator, source


def substitute(surface, offset_one, factor_one, upper_offset, upper_factor):
    level_one = offset_one + factor_one * surface

    def one_level(below_value, layer_data):
        value = layer_data[0] + layer_data[1] * below_value
        return value, value

    unused, higher = lax.scan(one_level, level_one, (upper_offset, upper_factor), unroll=4)
    return jnp.concatenate([surface[None], level_one[None], higher], axis=0)


def reference(column_old, coupling, sea_temp, land_mask, tile_weight, tile_coeff, tile_capacity, tile_conduct, tile_old, tile_forcing):
    smooth = (jnp.roll(coupling, 1, axis=1) + 2.0 * coupling + jnp.roll(coupling, -1, axis=1)) * 0.25
    offset_two, factor_two, upper_offset, upper_factor = eliminate_upper(column_old, smooth)
    land_a, land_b, denominator, source = tile_sums(tile_weight, tile_coeff, tile_capacity, tile_conduct, tile_old, tile_forcing)
    blocks = N_LON * N_LEV
    slot_count = COLS_DEV // N_LON
    mask_blocks = land_mask.reshape(blocks, COLS_DEV)
    land_rank = (jnp.cumsum(mask_blocks, axis=1) - 1).astype(jnp.int32)
    device = jnp.arange(blocks, dtype=jnp.int32)[:, None]
    lon_source = device // N_LEV
    lev_source = device % N_LEV
    owner_block = (land_rank % N_LON) * N_LEV + lev_source
    land_place = owner_block * COLS_DEV + lon_source * slot_count + land_rank // N_LON
    land_place = jnp.where(mask_blocks == 1, land_place, COLUMNS).reshape(COLUMNS).astype(jnp.int32)
    land_fetch = jnp.clip(land_place, 0, COLUMNS - 1).astype(jnp.int32)
    is_land = land_mask == 1
    column_a = jnp.where(is_land, land_a[land_fetch], sea_temp)
    column_b = jnp.where(is_land, land_b[land_fetch], jnp.ones_like(sea_temp))
    surface_flux = jnp.zeros_like(sea_temp)
    surface = jnp.zeros_like(sea_temp)
    offset_one = jnp.zeros_like(sea_temp)
    factor_one = jnp.zeros_like(sea_temp)
    for repeat in range(ITERS):
        p_surf, q_surf, offset_one, factor_one = lower_levels(column_old, smooth, offset_two, factor_two, surface_flux)
        surface = surface_solve(p_surf, q_surf, column_a, column_b)
        surface_flux = column_a - column_b * surface
    land_surface = jnp.zeros_like(sea_temp).at[land_place].set(surface, mode="drop")
    tile_temp = (source + tile_coeff * land_surface) / denominator
    column_temp = substitute(surface, offset_one, factor_one, upper_offset, upper_factor)
    return column_temp, tile_temp
```

```python
import functools

import jax
import jax.numpy as jnp
from jax import lax
from jax.experimental import pallas as pl
from jax.experimental.pallas import tpu as pltpu
from jax.sharding import PartitionSpec as P

ITERS = 8
LANES = 128
SUB = 8
GRANT = 16 * 1024 * 1024
HIGH = lax.Precision.HIGHEST
F32 = jnp.float32
I32 = jnp.int32
VMEM = pltpu.VMEM
DMA = pltpu.SemaphoreType.DMA


def on_chip(array):
    return pltpu.with_memory_space_constraint(array, pltpu.VMEM)


def chip_call(kernel, outs, in_spaces, out_spaces, scratch, args, cost):
    results = pl.pallas_call(
        kernel,
        out_shape=outs,
        in_specs=[pl.BlockSpec(memory_space=space) for space in in_spaces],
        out_specs=[pl.BlockSpec(memory_space=space) for space in out_spaces],
        scratch_shapes=scratch,
        cost_estimate=cost,
        compiler_params=pltpu.CompilerParams(vmem_limit_bytes=GRANT),
    )(*args)
    return [
        result if isinstance(out, jax.ShapeDtypeStruct) else on_chip(result)
        for result, out in zip(results, outs)
    ]


def lane_index(shape):
    return lax.broadcasted_iota(I32, shape, len(shape) - 1)


def row_index(shape):
    return lax.broadcasted_iota(I32, shape, len(shape) - 2)


def reciprocal(x):
    return 1.0 / x


def one_hot(condition):
    return jnp.where(condition, jnp.ones((), F32), jnp.zeros((), F32))


def dot(a, b):
    return jnp.dot(a, b, precision=HIGH, preferred_element_type=F32)


def lane_of(position, fast):
    return (position & 7) * 16 + (position >> 3) if fast else position


def position_of(lane, fast):
    return (lane & 15) * 8 + (lane >> 4) if fast else lane


def rank_row_of(row, fast):
    return (row & 7) * 8 + (row >> 3) if fast else row


def exchange(blocks):
    group = lane_index((SUB, LANES)) >> 4
    step = 1
    while step < SUB:
        high = (group & step) != 0
        done = list(blocks)
        for low in range(SUB):
            if low & step:
                continue
            a, b = blocks[low], blocks[low + step]
            done[low] = jnp.where(high, pltpu.roll(b, 16 * step, 1), a)
            done[low + step] = jnp.where(high, b, pltpu.roll(a, LANES - 16 * step, 1))
        blocks = done
        step *= 2
    return blocks


def build_tables(fast, mask, source_ref, first_ref, second_ref, place_ref, fetch_ref, spot_ref):
    rows = mask.shape[0]
    shape = (rows, LANES)
    land = mask.astype(F32)
    upper = one_hot(row_index((LANES, LANES)) <= lane_index((LANES, LANES)))
    running = dot(land, upper)
    totals = dot(land, jnp.ones((LANES, LANES), F32))
    before = one_hot(lane_index((rows, rows)) < row_index((rows, rows)))
    base = dot(before, totals).astype(I32)
    totals = totals.astype(I32)
    running = running.astype(I32)
    start = base & (LANES - 1)
    position = position_of(lane_index(shape), fast)
    ordinal = (position - start) & (LANES - 1)
    source = jnp.zeros(shape, I32)
    step = LANES // 2
    while step:
        reached = jnp.take_along_axis(running, source + (step - 1), axis=1)
        source = jnp.where(reached <= ordinal, source + step, source)
        step //= 2
    source_ref[...] = source
    valid = ordinal < totals
    first_ref[...] = one_hot(valid & (position >= start))
    second_ref[...] = one_hot(valid & (position < start))
    row_totals = lax.dot_general(
        jnp.ones((SUB, LANES), F32),
        land,
        (((1,), (1,)), ((), ())),
        precision=HIGH,
        preferred_element_type=F32,
    )
    earlier = one_hot(row_index((rows, rows)) < lane_index((rows, rows)))
    base_row = dot(row_totals, earlier).astype(I32)[:1]
    lead_row = jnp.broadcast_to(base_row >> 7, (rows, rows))
    wanted = rank_row_of(row_index((rows, rows)), fast)
    place_ref[...] = jnp.concatenate(
        [one_hot(lead_row == wanted), one_hot(lead_row + 1 == wanted)], axis=1
    )
    lead = (base >> 7)[:, :rows] if rows <= LANES else base[:, :1] >> 7
    held = rank_row_of(lane_index((rows, rows)), fast)
    fetch_ref[...] = jnp.concatenate(
        [one_hot(lead == held), one_hot(lead + 1 == held)], axis=0
    )
    spot = start + running - 1
    spot_ref[...] = lane_of(spot & (LANES - 1), fast) + (spot & LANES)


def prepare(
    fast,
    coupling,
    column_old,
    mask,
    smooth,
    old,
    source,
    first,
    second,
    place,
    fetch,
    spot,
    padded,
    sem_coupling,
    sem_old,
):
    levels, rows, lanes = smooth.shape
    blocks = rows // SUB
    inner = padded.at[:, pl.ds(SUB, rows), :]
    for t in range(rows):
        pltpu.make_async_copy(
            coupling.at[:, pl.ds(t * LANES, LANES)], padded.at[:, SUB + t, :], sem_coupling
        ).start()
    for t in range(rows):
        pltpu.make_async_copy(
            column_old.at[:, pl.ds(t * LANES, LANES)], old.at[:, t, :], sem_old
        ).start()
    blank = jnp.zeros((SUB, LANES), F32)

    def clear(level, carried):
        padded[level, pl.ds(0, SUB), :] = blank
        padded[level, pl.ds(SUB + rows, SUB), :] = blank
        return carried

    lax.fori_loop(0, levels, clear, 0)
    build_tables(fast, mask[...], source, first, second, place, fetch, spot)
    lane = lane_index((SUB, LANES))
    at_last = lane == LANES - 1
    at_first = lane == 0
    pltpu.make_async_copy(inner, inner, sem_coupling).wait()

    def smooth_level(level, carried):
        for g in range(blocks):
            here = padded[level, pl.ds(SUB + g * SUB, SUB), :]
            above = padded[level, pl.ds(SUB + g * SUB - 1, SUB), :]
            below = padded[level, pl.ds(SUB + g * SUB + 1, SUB), :]
            left = pltpu.roll(jnp.where(at_last, above, here), 1, 1)
            right = pltpu.roll(jnp.where(at_first, below, here), LANES - 1, 1)
            smooth[level, pl.ds(g * SUB, SUB), :] = (left + 2.0 * here + right) * 0.25
        return carried

    lax.fori_loop(0, levels, smooth_level, 0)
    pltpu.make_async_copy(old, old, sem_old).wait()


def eliminate(
    fast,
    parity,
    smooth,
    old,
    pair_edge,
    next_edge,
    source,
    first,
    second,
    place,
    tile_weight,
    tile_coeff,
    tile_capacity,
    tile_conduct,
    tile_old,
    tile_forcing,
    offset,
    factor,
    params,
    land,
    tile_base,
    tile_slope,
    send,
    low_edge,
    high_edge,
    weight,
    coeff,
    capacity,
    conduct,
    before,
    forcing,
    sems,
):
    levels, rows, lanes = smooth.shape
    blocks = rows // SUB
    copies = [
        pltpu.make_async_copy(source_tile, buffer, sems.at[n])
        for n, (source_tile, buffer) in enumerate(
            (
                (tile_weight, weight),
                (tile_coeff, coeff),
                (tile_capacity, capacity),
                (tile_conduct, conduct),
                (tile_old, before),
                (tile_forcing, forcing),
            )
        )
    ]
    for copy in copies:
        copy.start()
    even = parity[0] == 0
    pair, following = pair_edge[...], next_edge[...]
    low_edge[...] = pltpu.roll(jnp.where(even, following, pair), 1, 1) * 0.25
    high_edge[...] = pltpu.roll(jnp.where(even, pair, following), LANES - 1, 1) * 0.25
    row, lane = row_index((SUB, LANES)), lane_index((SUB, LANES))
    low_corner = (row == 0) & (lane == 0)
    high_corner = (row == SUB - 1) & (lane == LANES - 1)
    blank = jnp.zeros((SUB, LANES), F32)

    def smooth_at(level):
        values = [smooth[level, pl.ds(g * SUB, SUB), :] for g in range(blocks)]
        low = jnp.broadcast_to(low_edge[pl.ds(level, 1), :], (SUB, LANES))
        high = jnp.broadcast_to(high_edge[pl.ds(level, 1), :], (SUB, LANES))
        values[0] = values[0] + jnp.where(low_corner, low, blank)
        values[-1] = values[-1] + jnp.where(high_corner, high, blank)
        return values

    def step(count, carried):
        level = levels - count
        conduct_u, right_n = carried
        below = smooth_at(level - 1)
        next_u, next_n = [], []
        for g in range(blocks):
            inverse = reciprocal(conduct_u[g] + below[g])
            e = right_n[g] * inverse
            offset[level - 2, pl.ds(g * SUB, SUB), :] = e
            factor[level - 2, pl.ds(g * SUB, SUB), :] = below[g] * inverse
            next_u.append(1.0 + (below[g] * conduct_u[g]) * inverse)
            next_n.append(old[level - 1, pl.ds(g * SUB, SUB), :] + below[g] * e)
        return next_u, next_n

    top = [old[levels, pl.ds(g * SUB, SUB), :] for g in range(blocks)]
    ones = [jnp.ones((SUB, LANES), F32) for _ in range(blocks)]
    conduct_u, right_n = lax.fori_loop(0, levels - 1, step, (ones, top), unroll=2)
    ground = smooth_at(0)
    for g in range(blocks):
        here = pl.ds(g * SUB, SUB)
        params[0, here, :] = old[0, here, :]
        params[1, here, :] = right_n[g]
        params[2, here, :] = conduct_u[g]
        params[3, here, :] = ground[g]
    for copy in copies:
        copy.wait()
    tiles = weight.shape[0]

    def tile_block(g, carried):
        columns = pl.ds(pl.multiple_of(g * SUB * LANES, SUB * LANES), SUB * LANES)
        here = pl.ds(pl.multiple_of(g * SUB, SUB), SUB)
        weight_sum = land_a = land_b = blank
        for t in range(tiles):
            w, c, cap, con, was, force = (
                buffer[t, columns].reshape(SUB, LANES)
                for buffer in (weight, coeff, capacity, conduct, before, forcing)
            )
            keep = cap + con
            inverse = reciprocal(keep + c)
            src = cap * was + force
            slope = c * inverse
            tile_base[t, here, :] = src * inverse
            tile_slope[t, here, :] = slope
            share = w * slope
            weight_sum = weight_sum + w
            land_a = land_a + share * src
            land_b = land_b + share * keep
        inverse = reciprocal(weight_sum)
        land[0, here, :] = land_a * inverse
        land[1, here, :] = land_b * inverse
        return carried

    lax.fori_loop(0, blocks, tile_block, 0)
    pick, lead, rest = source[...], first[...], second[...]
    halves = []
    for n in range(4):
        moved = jnp.take_along_axis(params[n], pick, axis=1)
        halves.append(jnp.concatenate([moved * lead, moved * rest], axis=0))
    packed = dot(place[...], jnp.concatenate(halves, axis=1))
    for n in range(4):
        field = packed[:, n * LANES : (n + 1) * LANES]
        if fast:
            for k, block in enumerate(exchange([field[g * SUB : (g + 1) * SUB] for g in range(blocks)])):
                send[k, 2 + n] = block
        else:
            send[n] = field
    if fast:
        for k in range(blocks):
            for n in range(2):
                send[k, n] = land[n, pl.ds(k * SUB, SUB), :]


def finish(
    fast,
    inbox,
    slots,
    offset,
    factor,
    params,
    land,
    tile_base,
    tile_slope,
    fetch,
    spot,
    mask,
    sea,
    column_temp,
    tile_temp,
    solved,
    warm,
    column_buffer,
    tile_buffer,
    sems,
    tile_sem,
):
    upper, rows, lanes = offset.shape
    blocks = rows // SUB
    levels = upper + 2
    tiles = tile_base.shape[0]
    fields = []
    for n in range(2):
        if fast:
            fields.append(
                jnp.concatenate(exchange([inbox[k, n] for k in range(blocks)]), axis=0)
            )
        else:
            fields.append(inbox[n])
    windows = dot(fetch[...], jnp.concatenate(fields, axis=1))
    place = spot[...]
    lane, upper_half = place & (LANES - 1), place >= LANES
    is_land = mask[...] == 1
    for n, ocean in ((0, sea[...]), (1, jnp.ones((rows, LANES), F32))):
        one = windows[:rows, n * LANES : (n + 1) * LANES]
        two = windows[rows:, n * LANES : (n + 1) * LANES]
        found = jnp.where(
            upper_half,
            jnp.take_along_axis(two, lane, axis=1),
            jnp.take_along_axis(one, lane, axis=1),
        )
        solved[n, pl.ds(0, rows), :] = jnp.where(is_land, found, ocean)
        solved[n, pl.ds(rows, rows), :] = land[n]
    for n in range(4):
        solved[2 + n, pl.ds(0, rows), :] = params[n]
        for i in range(blocks):
            got = inbox[i, 2 + n] if fast else slots[n, pl.ds(i * SUB, SUB), :]
            solved[2 + n, pl.ds(rows + i * SUB, SUB), :] = got
    everything = 2 * blocks

    def iterate(repeat, flux):
        fluxes = []
        for g in range(everything):
            here = pl.ds(g * SUB, SUB)
            a, b = solved[0, here, :], solved[1, here, :]
            base, n1, w, ground = (solved[2 + n, here, :] for n in range(4))
            if g >= blocks:
                w = jnp.where(ground > 0.0, w, 1.0)
            k = ground * (1.0 + 0.5 * jnp.tanh(flux[g]))
            total = w + k
            top = (base + a) * total + k * n1
            bottom = (1.0 + b) * total + w * k
            surface = top * reciprocal(bottom)
            if g >= blocks:
                warm[pl.ds((g - blocks) * SUB, SUB), :] = jnp.where(ground > 0.0, surface, 0.0)
            else:
                column_buffer[0, here, :] = surface
                column_buffer[1, here, :] = k
            fluxes.append(a - b * surface)
        return fluxes

    zero = jnp.zeros((SUB, LANES), F32)
    lax.fori_loop(0, ITERS, iterate, [zero] * everything)
    for t in range(tiles):
        tile_buffer[t] = tile_base[t] + tile_slope[t] * warm[...]
    for t in range(rows):
        pltpu.make_async_copy(
            tile_buffer.at[:, t, :], tile_temp.at[:, pl.ds(t * LANES, LANES)], tile_sem
        ).start()
    width = 2
    for part in range(blocks // width):
        spans = [pl.ds((part * width + g) * SUB, SUB) for g in range(width)]
        values = []
        for here in spans:
            surface, k = column_buffer[0, here, :], column_buffer[1, here, :]
            n1, w = params[1, here, :], params[2, here, :]
            value = (n1 + k * surface) * reciprocal(w + k)
            column_buffer[1, here, :] = value
            values.append(value)

        def substitute(level, values):
            values = [
                offset[level, here, :] + factor[level, here, :] * value
                for here, value in zip(spans, values)
            ]
            for here, value in zip(spans, values):
                column_buffer[level + 2, here, :] = value
            return values

        lax.fori_loop(0, upper, substitute, values, unroll=4)
        for t in range(part * width * SUB, (part + 1) * width * SUB):
            pltpu.make_async_copy(
                column_buffer.at[:, t, :],
                column_temp.at[:, pl.ds(t * LANES, LANES)],
                sems.at[part],
            ).start()
    pltpu.make_async_copy(tile_buffer, tile_buffer, tile_sem).wait()
    for part in range(blocks // width):
        span = column_buffer.at[:, pl.ds(part * width * SUB, width * SUB), :]
        pltpu.make_async_copy(span, span, sems.at[part]).wait()


def on_device(
    column_old,
    coupling,
    sea_temp,
    land_mask,
    tile_weight,
    tile_coeff,
    tile_capacity,
    tile_conduct,
    tile_old,
    tile_forcing,
):
    axes = ("lon", "lev")
    couplings, columns = coupling.shape
    levels = column_old.shape[0]
    tiles = tile_weight.shape[0]
    peers = lax.axis_size("lon")
    slot_count = columns // peers
    rows = columns // LANES
    blocks = rows // SUB
    fast = peers == SUB and rows == SUB * SUB
    devices = peers * lax.axis_size("lev")
    parity = lax.rem(lax.axis_index(axes), 2)
    first_edge, last_edge = coupling[:, :LANES], coupling[:, columns - LANES :]
    even = parity == 0
    pairs = [(i, i ^ 1) for i in range(devices)]
    following = [(i, (i + 1 if i % 2 else i - 1) % devices) for i in range(devices)]
    next_edge = lax.ppermute(jnp.where(even, first_edge, last_edge), axes, following)
    pair_edge = lax.ppermute(jnp.where(even, last_edge, first_edge), axes, pairs)

    hbm, vmem, smem = pl.ANY, pltpu.VMEM, pltpu.SMEM
    full = (rows, LANES)
    mask = land_mask.reshape(full)
    table_outs = [
        VMEM(full, I32),
        VMEM(full, F32),
        VMEM(full, F32),
        VMEM((rows, 2 * rows), F32),
        VMEM((2 * rows, rows), F32),
        VMEM(full, I32),
    ]
    smooth, old, source, first, second, place, fetch, spot = chip_call(
        functools.partial(prepare, fast),
        [VMEM((couplings,) + full, F32), VMEM((levels,) + full, F32)] + table_outs,
        [hbm, hbm, vmem],
        [vmem] * 8,
        [VMEM((couplings, rows + 2 * SUB, LANES), F32), DMA, DMA],
        (coupling, column_old, mask),
        pl.CostEstimate(
            flops=8 * couplings * columns, bytes_accessed=8 * levels * columns, transcendentals=0
        ),
    )
    sent = (peers, 6, SUB, LANES) if fast else (4,) + full
    handed = VMEM if fast else jax.ShapeDtypeStruct
    offset, factor, params, land, tile_base, tile_slope, send = chip_call(
        functools.partial(eliminate, fast),
        [
            VMEM((levels - 2,) + full, F32),
            VMEM((levels - 2,) + full, F32),
            VMEM((4,) + full, F32),
            handed((2,) + full, F32),
            VMEM((tiles,) + full, F32),
            VMEM((tiles,) + full, F32),
            handed(sent, F32),
        ],
        [smem] + [vmem] * 8 + [hbm] * 6,
        [vmem] * 7,
        [VMEM((couplings, LANES), F32)] * 2 + [VMEM((tiles, columns), F32)] * 6 + [DMA((6,))],
        (
            parity.reshape(1),
            smooth,
            old,
            pair_edge,
            next_edge,
            source,
            first,
            second,
            place,
            tile_weight,
            tile_coeff,
            tile_capacity,
            tile_conduct,
            tile_old,
            tile_forcing,
        ),
        pl.CostEstimate(
            flops=20 * levels * columns, bytes_accessed=24 * tiles * columns, transcendentals=0
        ),
    )
    if fast:
        inbox = lax.all_to_all(send, "lon", split_axis=0, concat_axis=0, tiled=True)
        slots = inbox
    else:
        ranked = send.reshape(4, slot_count, peers).transpose(2, 0, 1)
        own = land.reshape(2, peers, slot_count).transpose(1, 0, 2)
        got = lax.all_to_all(
            jnp.concatenate([own, ranked], axis=1), "lon", split_axis=0, concat_axis=0, tiled=True
        )
        inbox = got[:, :2].transpose(1, 2, 0).reshape((2,) + full)
        slots = got[:, 2:].transpose(1, 0, 2).reshape((4,) + full)
    width = 2
    column_temp, tile_temp = chip_call(
        functools.partial(finish, fast),
        [
            jax.ShapeDtypeStruct(column_old.shape, F32),
            jax.ShapeDtypeStruct(tile_old.shape, F32),
        ],
        [vmem] * 12,
        [hbm, hbm],
        [
            VMEM((6, 2 * rows, LANES), F32),
            VMEM(full, F32),
            VMEM((levels,) + full, F32),
            VMEM((tiles,) + full, F32),
            DMA((blocks // width,)),
            DMA,
        ],
        (
            inbox,
            slots,
            offset,
            factor,
            params,
            land,
            tile_base,
            tile_slope,
            fetch,
            spot,
            mask,
            sea_temp.reshape(full),
        ),
        pl.CostEstimate(
            flops=4 * levels * columns, bytes_accessed=4 * levels * columns, transcendentals=0
        ),
    )
    return column_temp, tile_temp


def solution(mesh):
    wide, flat = P(None, ("lon", "lev")), P(("lon", "lev"))
    in_specs = (wide, wide, flat, flat) + (wide,) * 6
    return jax.shard_map(
        on_device, mesh=mesh, in_specs=in_specs, out_specs=(wide, wide), check_vma=False
    )
```

```python
import functools

import jax
import jax.numpy as jnp
from jax import lax
from jax.experimental import pallas as pl
from jax.experimental.pallas import tpu as pltpu
from jax.sharding import PartitionSpec as P

ITERS = 8
LANES = 128
SUB = 8
GRANT = 16 * 1024 * 1024
WIDE_GRANT = 55 * 1024 * 1024
HIGH = lax.Precision.HIGHEST
F32 = jnp.float32
I32 = jnp.int32
VMEM = pltpu.VMEM
DMA = pltpu.SemaphoreType.DMA


def on_chip(array):
    return pltpu.with_memory_space_constraint(array, pltpu.VMEM)


def chip_call(kernel, outs, in_spaces, out_spaces, scratch, args, cost, grant=GRANT):
    results = pl.pallas_call(
        kernel,
        out_shape=outs,
        in_specs=[pl.BlockSpec(memory_space=space) for space in in_spaces],
        out_specs=[pl.BlockSpec(memory_space=space) for space in out_spaces],
        scratch_shapes=scratch,
        cost_estimate=cost,
        compiler_params=pltpu.CompilerParams(vmem_limit_bytes=grant),
    )(*args)
    return [
        result if isinstance(out, jax.ShapeDtypeStruct) else on_chip(result)
        for result, out in zip(results, outs)
    ]


def lane_index(shape):
    return lax.broadcasted_iota(I32, shape, len(shape) - 1)


def row_index(shape):
    return lax.broadcasted_iota(I32, shape, len(shape) - 2)


def reciprocal(x):
    return 1.0 / x


def one_hot(condition):
    return jnp.where(condition, jnp.ones((), F32), jnp.zeros((), F32))


def dot(a, b):
    return jnp.dot(a, b, precision=HIGH, preferred_element_type=F32)


def lane_of(position, fast):
    return (position & 7) * 16 + (position >> 3) if fast else position


def position_of(lane, fast):
    return (lane & 15) * 8 + (lane >> 4) if fast else lane


def rank_row_of(row, fast):
    return (row & 7) * 8 + (row >> 3) if fast else row


def exchange(blocks):
    group = lane_index((SUB, LANES)) >> 4
    step = 1
    while step < SUB:
        high = (group & step) != 0
        done = list(blocks)
        for low in range(SUB):
            if low & step:
                continue
            a, b = blocks[low], blocks[low + step]
            done[low] = jnp.where(high, pltpu.roll(b, 16 * step, 1), a)
            done[low + step] = jnp.where(high, b, pltpu.roll(a, LANES - 16 * step, 1))
        blocks = done
        step *= 2
    return blocks


def build_tables(fast, mask, source_ref, first_ref, second_ref, place_ref, fetch_ref, spot_ref):
    rows = mask.shape[0]
    shape = (rows, LANES)
    land = mask.astype(F32)
    upper = one_hot(row_index((LANES, LANES)) <= lane_index((LANES, LANES)))
    running = dot(land, upper)
    totals = dot(land, jnp.ones((LANES, LANES), F32))
    before = one_hot(lane_index((rows, rows)) < row_index((rows, rows)))
    base = dot(before, totals).astype(I32)
    totals = totals.astype(I32)
    running = running.astype(I32)
    start = base & (LANES - 1)
    position = position_of(lane_index(shape), fast)
    ordinal = (position - start) & (LANES - 1)
    source = jnp.zeros(shape, I32)
    step = LANES // 2
    while step:
        reached = jnp.take_along_axis(running, source + (step - 1), axis=1)
        source = jnp.where(reached <= ordinal, source + step, source)
        step //= 2
    source_ref[...] = source
    valid = ordinal < totals
    first_ref[...] = one_hot(valid & (position >= start))
    second_ref[...] = one_hot(valid & (position < start))
    row_totals = lax.dot_general(
        jnp.ones((SUB, LANES), F32),
        land,
        (((1,), (1,)), ((), ())),
        precision=HIGH,
        preferred_element_type=F32,
    )
    earlier = one_hot(row_index((rows, rows)) < lane_index((rows, rows)))
    base_row = dot(row_totals, earlier).astype(I32)[:1]
    lead_row = jnp.broadcast_to(base_row >> 7, (rows, rows))
    wanted = rank_row_of(row_index((rows, rows)), fast)
    place_ref[...] = jnp.concatenate(
        [one_hot(lead_row == wanted), one_hot(lead_row + 1 == wanted)], axis=1
    )
    lead = (base >> 7)[:, :rows] if rows <= LANES else base[:, :1] >> 7
    held = rank_row_of(lane_index((rows, rows)), fast)
    fetch_ref[...] = jnp.concatenate(
        [one_hot(lead == held), one_hot(lead + 1 == held)], axis=0
    )
    spot = start + running - 1
    spot_ref[...] = lane_of(spot & (LANES - 1), fast) + (spot & LANES)


def prepare(
    fast,
    coupling,
    column_old,
    mask,
    smooth,
    old,
    source,
    first,
    second,
    place,
    fetch,
    spot,
    padded,
    sem_coupling,
    sem_old,
):
    levels, rows, lanes = smooth.shape
    blocks = rows // SUB
    inner = padded.at[:, pl.ds(SUB, rows), :]
    for t in range(rows):
        pltpu.make_async_copy(
            coupling.at[:, pl.ds(t * LANES, LANES)], padded.at[:, SUB + t, :], sem_coupling
        ).start()
    for t in range(rows):
        pltpu.make_async_copy(
            column_old.at[:, pl.ds(t * LANES, LANES)], old.at[:, t, :], sem_old
        ).start()
    blank = jnp.zeros((SUB, LANES), F32)

    def clear(level, carried):
        padded[level, pl.ds(0, SUB), :] = blank
        padded[level, pl.ds(SUB + rows, SUB), :] = blank
        return carried

    lax.fori_loop(0, levels, clear, 0, unroll=3)
    build_tables(fast, mask[...], source, first, second, place, fetch, spot)
    lane = lane_index((SUB, LANES))
    at_last = lane == LANES - 1
    at_first = lane == 0
    pltpu.make_async_copy(inner, inner, sem_coupling).wait()

    def smooth_level(level, carried):
        for g in range(blocks):
            here = padded[level, pl.ds(SUB + g * SUB, SUB), :]
            above = padded[level, pl.ds(SUB + g * SUB - 1, SUB), :]
            below = padded[level, pl.ds(SUB + g * SUB + 1, SUB), :]
            left = pltpu.roll(jnp.where(at_last, above, here), 1, 1)
            right = pltpu.roll(jnp.where(at_first, below, here), LANES - 1, 1)
            smooth[level, pl.ds(g * SUB, SUB), :] = (left + 2.0 * here + right) * 0.25
        return carried

    lax.fori_loop(0, levels, smooth_level, 0, unroll=levels // 3)
    pltpu.make_async_copy(old, old, sem_old).wait()


def eliminate(
    fast,
    parity,
    smooth,
    old,
    pair_edge,
    next_edge,
    source,
    first,
    second,
    place,
    tile_weight,
    tile_coeff,
    tile_capacity,
    tile_conduct,
    tile_old,
    tile_forcing,
    offset,
    factor,
    params,
    land,
    tile_base,
    tile_slope,
    send,
    low_edge,
    high_edge,
    weight,
    coeff,
    capacity,
    conduct,
    before,
    forcing,
    sems,
):
    levels, rows, lanes = smooth.shape
    blocks = rows // SUB
    copies = [
        pltpu.make_async_copy(source_tile, buffer, sems.at[n])
        for n, (source_tile, buffer) in enumerate(
            (
                (tile_weight, weight),
                (tile_coeff, coeff),
                (tile_capacity, capacity),
                (tile_conduct, conduct),
                (tile_old, before),
                (tile_forcing, forcing),
            )
        )
    ]
    for copy in copies:
        copy.start()
    even = parity[0] == 0
    pair, following = pair_edge[...], next_edge[...]
    low_edge[...] = pltpu.roll(jnp.where(even, following, pair), 1, 1) * 0.25
    high_edge[...] = pltpu.roll(jnp.where(even, pair, following), LANES - 1, 1) * 0.25
    row, lane = row_index((SUB, LANES)), lane_index((SUB, LANES))
    low_corner = (row == 0) & (lane == 0)
    high_corner = (row == SUB - 1) & (lane == LANES - 1)
    blank = jnp.zeros((SUB, LANES), F32)

    def smooth_at(level):
        values = [smooth[level, pl.ds(g * SUB, SUB), :] for g in range(blocks)]
        low = jnp.broadcast_to(low_edge[pl.ds(level, 1), :], (SUB, LANES))
        high = jnp.broadcast_to(high_edge[pl.ds(level, 1), :], (SUB, LANES))
        values[0] = values[0] + jnp.where(low_corner, low, blank)
        values[-1] = values[-1] + jnp.where(high_corner, high, blank)
        return values

    def step(count, carried):
        level = levels - count
        conduct_u, right_n = carried
        below = smooth_at(level - 1)
        next_u, next_n = [], []
        for g in range(blocks):
            inverse = reciprocal(conduct_u[g] + below[g])
            e = right_n[g] * inverse
            offset[level - 2, pl.ds(g * SUB, SUB), :] = e
            factor[level - 2, pl.ds(g * SUB, SUB), :] = below[g] * inverse
            next_u.append(1.0 + (below[g] * conduct_u[g]) * inverse)
            next_n.append(old[level - 1, pl.ds(g * SUB, SUB), :] + below[g] * e)
        return next_u, next_n

    top = [old[levels, pl.ds(g * SUB, SUB), :] for g in range(blocks)]
    ones = [jnp.ones((SUB, LANES), F32) for _ in range(blocks)]
    conduct_u, right_n = lax.fori_loop(0, levels - 1, step, (ones, top), unroll=2)
    ground = smooth_at(0)
    for g in range(blocks):
        here = pl.ds(g * SUB, SUB)
        params[0, here, :] = old[0, here, :]
        params[1, here, :] = right_n[g]
        params[2, here, :] = conduct_u[g]
        params[3, here, :] = ground[g]
    for copy in copies:
        copy.wait()
    tiles = weight.shape[0]

    def tile_block(g, carried):
        columns = pl.ds(pl.multiple_of(g * SUB * LANES, SUB * LANES), SUB * LANES)
        here = pl.ds(pl.multiple_of(g * SUB, SUB), SUB)
        weight_sum = land_a = land_b = blank
        for t in range(tiles):
            w, c, cap, con, was, force = (
                buffer[t, columns].reshape(SUB, LANES)
                for buffer in (weight, coeff, capacity, conduct, before, forcing)
            )
            keep = cap + con
            inverse = reciprocal(keep + c)
            src = cap * was + force
            slope = c * inverse
            tile_base[t, here, :] = src * inverse
            tile_slope[t, here, :] = slope
            share = w * slope
            weight_sum = weight_sum + w
            land_a = land_a + share * src
            land_b = land_b + share * keep
        inverse = reciprocal(weight_sum)
        land[0, here, :] = land_a * inverse
        land[1, here, :] = land_b * inverse
        return carried

    lax.fori_loop(0, blocks, tile_block, 0)
    pick, lead, rest = source[...], first[...], second[...]
    halves = []
    for n in range(4):
        moved = jnp.take_along_axis(params[n], pick, axis=1)
        halves.append(jnp.concatenate([moved * lead, moved * rest], axis=0))
    packed = dot(place[...], jnp.concatenate(halves, axis=1))
    for n in range(4):
        field = packed[:, n * LANES : (n + 1) * LANES]
        if fast:
            for k, block in enumerate(exchange([field[g * SUB : (g + 1) * SUB] for g in range(blocks)])):
                send[k, 2 + n] = block
        else:
            send[n] = field
    if fast:
        for k in range(blocks):
            for n in range(2):
                send[k, n] = land[n, pl.ds(k * SUB, SUB), :]


def finish(
    fast,
    inbox,
    slots,
    offset,
    factor,
    params,
    land,
    tile_base,
    tile_slope,
    fetch,
    spot,
    mask,
    sea,
    column_temp,
    tile_temp,
    solved,
    warm,
    column_buffer,
    tile_buffer,
    sems,
    tile_sem,
):
    upper, rows, lanes = offset.shape
    blocks = rows // SUB
    levels = upper + 2
    tiles = tile_base.shape[0]
    fields = []
    for n in range(2):
        if fast:
            fields.append(
                jnp.concatenate(exchange([inbox[k, n] for k in range(blocks)]), axis=0)
            )
        else:
            fields.append(inbox[n])
    windows = dot(fetch[...], jnp.concatenate(fields, axis=1))
    place = spot[...]
    lane, upper_half = place & (LANES - 1), place >= LANES
    is_land = mask[...] == 1
    for n, ocean in ((0, sea[...]), (1, jnp.ones((rows, LANES), F32))):
        one = windows[:rows, n * LANES : (n + 1) * LANES]
        two = windows[rows:, n * LANES : (n + 1) * LANES]
        found = jnp.where(
            upper_half,
            jnp.take_along_axis(two, lane, axis=1),
            jnp.take_along_axis(one, lane, axis=1),
        )
        solved[n, pl.ds(0, rows), :] = jnp.where(is_land, found, ocean)
        solved[n, pl.ds(rows, rows), :] = land[n]
    for n in range(4):
        solved[2 + n, pl.ds(0, rows), :] = params[n]
        for i in range(blocks):
            got = inbox[i, 2 + n] if fast else slots[n, pl.ds(i * SUB, SUB), :]
            solved[2 + n, pl.ds(rows + i * SUB, SUB), :] = got
    everything = 2 * blocks

    def iterate(repeat, flux):
        fluxes = []
        for g in range(everything):
            here = pl.ds(g * SUB, SUB)
            a, b = solved[0, here, :], solved[1, here, :]
            base, n1, w, ground = (solved[2 + n, here, :] for n in range(4))
            if g >= blocks:
                w = jnp.where(ground > 0.0, w, 1.0)
            k = ground * (1.0 + 0.5 * jnp.tanh(flux[g]))
            total = w + k
            top = (base + a) * total + k * n1
            bottom = (1.0 + b) * total + w * k
            surface = top * reciprocal(bottom)
            if g >= blocks:
                warm[pl.ds((g - blocks) * SUB, SUB), :] = jnp.where(ground > 0.0, surface, 0.0)
            else:
                column_buffer[0, here, :] = surface
                column_buffer[1, here, :] = k
            fluxes.append(a - b * surface)
        return fluxes

    zero = jnp.zeros((SUB, LANES), F32)
    lax.fori_loop(0, ITERS, iterate, [zero] * everything)
    for t in range(tiles):
        tile_buffer[t] = tile_base[t] + tile_slope[t] * warm[...]
    for t in range(rows):
        pltpu.make_async_copy(
            tile_buffer.at[:, t, :], tile_temp.at[:, pl.ds(t * LANES, LANES)], tile_sem
        ).start()
    width = 2
    for part in range(blocks // width):
        spans = [pl.ds((part * width + g) * SUB, SUB) for g in range(width)]
        values = []
        for here in spans:
            surface, k = column_buffer[0, here, :], column_buffer[1, here, :]
            n1, w = params[1, here, :], params[2, here, :]
            value = (n1 + k * surface) * reciprocal(w + k)
            column_buffer[1, here, :] = value
            values.append(value)

        def substitute(level, values):
            values = [
                offset[level, here, :] + factor[level, here, :] * value
                for here, value in zip(spans, values)
            ]
            for here, value in zip(spans, values):
                column_buffer[level + 2, here, :] = value
            return values

        lax.fori_loop(0, upper, substitute, values, unroll=4)
        for t in range(part * width * SUB, (part + 1) * width * SUB):
            pltpu.make_async_copy(
                column_buffer.at[:, t, :],
                column_temp.at[:, pl.ds(t * LANES, LANES)],
                sems.at[part],
            ).start()
    pltpu.make_async_copy(tile_buffer, tile_buffer, tile_sem).wait()
    for part in range(blocks // width):
        span = column_buffer.at[:, pl.ds(part * width * SUB, width * SUB), :]
        pltpu.make_async_copy(span, span, sems.at[part]).wait()


def on_device(
    column_old,
    coupling,
    sea_temp,
    land_mask,
    tile_weight,
    tile_coeff,
    tile_capacity,
    tile_conduct,
    tile_old,
    tile_forcing,
):
    axes = ("lon", "lev")
    couplings, columns = coupling.shape
    levels = column_old.shape[0]
    tiles = tile_weight.shape[0]
    peers = lax.axis_size("lon")
    slot_count = columns // peers
    rows = columns // LANES
    blocks = rows // SUB
    fast = peers == SUB and rows == SUB * SUB
    devices = peers * lax.axis_size("lev")
    parity = lax.rem(lax.axis_index(axes), 2)
    first_edge, last_edge = coupling[:, :LANES], coupling[:, columns - LANES :]
    even = parity == 0
    pairs = [(i, i ^ 1) for i in range(devices)]
    following = [(i, (i + 1 if i % 2 else i - 1) % devices) for i in range(devices)]
    next_edge = lax.ppermute(jnp.where(even, first_edge, last_edge), axes, following)
    pair_edge = lax.ppermute(jnp.where(even, last_edge, first_edge), axes, pairs)

    hbm, vmem, smem = pl.ANY, pltpu.VMEM, pltpu.SMEM
    full = (rows, LANES)
    mask = land_mask.reshape(full)
    table_outs = [
        VMEM(full, I32),
        VMEM(full, F32),
        VMEM(full, F32),
        VMEM((rows, 2 * rows), F32),
        VMEM((2 * rows, rows), F32),
        VMEM(full, I32),
    ]
    smooth, old, source, first, second, place, fetch, spot = chip_call(
        functools.partial(prepare, fast),
        [VMEM((couplings,) + full, F32), VMEM((levels,) + full, F32)] + table_outs,
        [hbm, hbm, vmem],
        [vmem] * 8,
        [VMEM((couplings, rows + 2 * SUB, LANES), F32), DMA, DMA],
        (coupling, column_old, mask),
        pl.CostEstimate(
            flops=8 * couplings * columns, bytes_accessed=8 * levels * columns, transcendentals=0
        ),
        WIDE_GRANT,
    )
    sent = (peers, 6, SUB, LANES) if fast else (4,) + full
    handed = VMEM if fast else jax.ShapeDtypeStruct
    offset, factor, params, land, tile_base, tile_slope, send = chip_call(
        functools.partial(eliminate, fast),
        [
            VMEM((levels - 2,) + full, F32),
            VMEM((levels - 2,) + full, F32),
            VMEM((4,) + full, F32),
            handed((2,) + full, F32),
            VMEM((tiles,) + full, F32),
            VMEM((tiles,) + full, F32),
            handed(sent, F32),
        ],
        [smem] + [vmem] * 8 + [hbm] * 6,
        [vmem] * 7,
        [VMEM((couplings, LANES), F32)] * 2 + [VMEM((tiles, columns), F32)] * 6 + [DMA((6,))],
        (
            parity.reshape(1),
            smooth,
            old,
            pair_edge,
            next_edge,
            source,
            first,
            second,
            place,
            tile_weight,
            tile_coeff,
            tile_capacity,
            tile_conduct,
            tile_old,
            tile_forcing,
        ),
        pl.CostEstimate(
            flops=20 * levels * columns, bytes_accessed=24 * tiles * columns, transcendentals=0
        ),
    )
    if fast:
        inbox = lax.all_to_all(send, "lon", split_axis=0, concat_axis=0, tiled=True)
        slots = inbox
    else:
        ranked = send.reshape(4, slot_count, peers).transpose(2, 0, 1)
        own = land.reshape(2, peers, slot_count).transpose(1, 0, 2)
        got = lax.all_to_all(
            jnp.concatenate([own, ranked], axis=1), "lon", split_axis=0, concat_axis=0, tiled=True
        )
        inbox = got[:, :2].transpose(1, 2, 0).reshape((2,) + full)
        slots = got[:, 2:].transpose(1, 0, 2).reshape((4,) + full)
    width = 2
    column_temp, tile_temp = chip_call(
        functools.partial(finish, fast),
        [
            jax.ShapeDtypeStruct(column_old.shape, F32),
            jax.ShapeDtypeStruct(tile_old.shape, F32),
        ],
        [vmem] * 12,
        [hbm, hbm],
        [
            VMEM((6, 2 * rows, LANES), F32),
            VMEM(full, F32),
            VMEM((levels,) + full, F32),
            VMEM((tiles,) + full, F32),
            DMA((blocks // width,)),
            DMA,
        ],
        (
            inbox,
            slots,
            offset,
            factor,
            params,
            land,
            tile_base,
            tile_slope,
            fetch,
            spot,
            mask,
            sea_temp.reshape(full),
        ),
        pl.CostEstimate(
            flops=4 * levels * columns, bytes_accessed=4 * levels * columns, transcendentals=0
        ),
    )
    return column_temp, tile_temp


def solution(mesh):
    wide, flat = P(None, ("lon", "lev")), P(("lon", "lev"))
    in_specs = (wide, wide, flat, flat) + (wide,) * 6
    return jax.shard_map(
        on_device, mesh=mesh, in_specs=in_specs, out_specs=(wide, wide), check_vma=False
    )
```

```python
import functools

import jax
import jax.numpy as jnp
from jax import lax
from jax.experimental import pallas as pl
from jax.experimental.pallas import tpu as pltpu
from jax.sharding import PartitionSpec as P


ITERS = 8
LANES = 128
SUB = 8
GRANT = 16 * 1024 * 1024
WIDE_GRANT = 55 * 1024 * 1024
EDGE_GRANT = 60 * 1024 * 1024
TILE_GRANT = 48 * 1024 * 1024
F32 = jnp.float32
I32 = jnp.int32
VMEM = pltpu.VMEM
DMA = pltpu.SemaphoreType.DMA


def on_chip(array):
    return pltpu.with_memory_space_constraint(array, pltpu.VMEM)


def chip_call(kernel, outs, in_spaces, out_spaces, scratch, args, cost, grant=GRANT):
    results = pl.pallas_call(
        kernel,
        out_shape=outs,
        in_specs=[pl.BlockSpec(memory_space=space) for space in in_spaces],
        out_specs=[pl.BlockSpec(memory_space=space) for space in out_spaces],
        scratch_shapes=scratch,
        cost_estimate=cost,
        compiler_params=pltpu.CompilerParams(vmem_limit_bytes=grant),
    )(*args)
    return [
        result if isinstance(out, jax.ShapeDtypeStruct) else on_chip(result)
        for result, out in zip(results, outs)
    ]


def lane_index(shape):
    return lax.broadcasted_iota(I32, shape, len(shape) - 1)


def row_index(shape):
    return lax.broadcasted_iota(I32, shape, len(shape) - 2)


def reciprocal(x):
    return 1.0 / x


def one_hot(condition):
    return jnp.where(condition, jnp.ones((), F32), jnp.zeros((), F32))


def spread(values):
    high = values.astype(jnp.bfloat16)
    rest = values - high.astype(F32)
    middle = rest.astype(jnp.bfloat16)
    low = (rest - middle.astype(F32)).astype(jnp.bfloat16)
    return jnp.concatenate([high, middle, low], axis=0)


def select_rows(chooser, values):
    return jnp.dot(chooser, spread(values), preferred_element_type=F32)


def count_dot(a, b):
    return jnp.dot(
        a.astype(jnp.bfloat16), b.astype(jnp.bfloat16), preferred_element_type=F32
    )


def lane_of(position, fast):
    return (position & 7) * 16 + (position >> 3) if fast else position


def position_of(lane, fast):
    return (lane & 15) * 8 + (lane >> 4) if fast else lane


def rank_row_of(row, fast):
    return (row & 7) * 8 + (row >> 3) if fast else row


def exchange(blocks):
    group = lane_index((SUB, LANES)) >> 4
    step = 1
    while step < SUB:
        high = (group & step) != 0
        done = list(blocks)
        for low in range(SUB):
            if low & step:
                continue
            a, b = blocks[low], blocks[low + step]
            done[low] = jnp.where(high, pltpu.roll(b, 16 * step, 1), a)
            done[low + step] = jnp.where(high, b, pltpu.roll(a, LANES - 16 * step, 1))
        blocks = done
        step *= 2
    return blocks


def build_tables(fast, mask, source_ref, first_ref, second_ref, place_ref, fetch_ref, spot_ref):
    rows = mask.shape[0]
    shape = (rows, LANES)
    land = mask.astype(F32)
    upper = one_hot(row_index((LANES, LANES)) <= lane_index((LANES, LANES)))
    running = count_dot(land, upper)
    totals = count_dot(land, jnp.ones((LANES, LANES), F32))
    before = one_hot(lane_index((rows, rows)) < row_index((rows, rows)))
    base = count_dot(before, totals).astype(I32)
    totals = totals.astype(I32)
    running = running.astype(I32)
    start = base & (LANES - 1)
    position = position_of(lane_index(shape), fast)
    ordinal = (position - start) & (LANES - 1)
    source = jnp.zeros(shape, I32)
    step = LANES // 2
    while step:
        reached = jnp.take_along_axis(running, source + (step - 1), axis=1)
        source = jnp.where(reached <= ordinal, source + step, source)
        step //= 2
    source_ref[...] = source
    valid = ordinal < totals
    first_ref[...] = one_hot(valid & (position >= start))
    second_ref[...] = one_hot(valid & (position < start))
    row_totals = lax.dot_general(
        jnp.ones((SUB, LANES), jnp.bfloat16),
        land.astype(jnp.bfloat16),
        (((1,), (1,)), ((), ())),
        preferred_element_type=F32,
    )
    earlier = one_hot(row_index((rows, rows)) < lane_index((rows, rows)))
    base_row = count_dot(row_totals, earlier).astype(I32)[:1]
    lead_row = jnp.broadcast_to(base_row >> 7, (rows, rows))
    wanted = rank_row_of(row_index((rows, rows)), fast)
    place_ref[...] = jnp.concatenate(
        [one_hot(lead_row == wanted), one_hot(lead_row + 1 == wanted)] * 3, axis=1
    ).astype(jnp.bfloat16)
    lead = (base >> 7)[:, :rows] if rows <= LANES else base[:, :1] >> 7
    held = rank_row_of(lane_index((rows, rows)), fast)
    chooser = jnp.concatenate([one_hot(lead == held), one_hot(lead + 1 == held)], axis=0)
    fetch_ref[...] = jnp.concatenate([chooser] * 3, axis=1).astype(jnp.bfloat16)
    spot = start + running - 1
    spot_ref[...] = lane_of(spot & (LANES - 1), fast) + (spot & LANES)


def cut_edges(parity, coupling, next_edge, pair_edge, low, high, sems):
    columns = coupling.shape[1]
    copies = [
        pltpu.make_async_copy(coupling.at[:, pl.ds(0, LANES)], low, sems.at[0]),
        pltpu.make_async_copy(coupling.at[:, pl.ds(columns - LANES, LANES)], high, sems.at[1]),
    ]
    for copy in copies:
        copy.start()
    for copy in copies:
        copy.wait()
    even = parity[0] == 0
    next_edge[...] = jnp.where(even, low[...], high[...])
    pair_edge[...] = jnp.where(even, high[...], low[...])


def prepare(
    fast, coupling, mask, padded, source, first, second, place, fetch, spot, held, sem, mask_sem
):
    levels, height, _ = padded.shape
    rows = height - 2 * SUB
    mask_copy = pltpu.make_async_copy(mask, held, mask_sem)
    mask_copy.start()
    for t in range(rows):
        pltpu.make_async_copy(
            coupling.at[:, pl.ds(t * LANES, LANES)], padded.at[:, SUB + t, :], sem
        ).start()
    blank = jnp.zeros((SUB, LANES), F32)

    def clear(level, carried):
        padded[level, pl.ds(0, SUB), :] = blank
        padded[level, pl.ds(SUB + rows, SUB), :] = blank
        return carried

    lax.fori_loop(0, levels, clear, 0, unroll=3)
    mask_copy.wait()
    build_tables(fast, held[...], source, first, second, place, fetch, spot)
    inner = padded.at[:, pl.ds(SUB, rows), :]
    pltpu.make_async_copy(inner, inner, sem).wait()


def eliminate(
    fast,
    parity,
    padded,
    old,
    pair_edge,
    next_edge,
    source,
    first,
    second,
    place,
    tile_weight,
    tile_coeff,
    tile_capacity,
    tile_conduct,
    tile_old,
    tile_forcing,
    offset,
    factor,
    params,
    land,
    tile_base,
    tile_slope,
    send,
    low_edge,
    high_edge,
    weight,
    coeff,
    capacity,
    conduct,
    before,
    forcing,
    sems,
):
    levels, height, _ = padded.shape
    rows = height - 2 * SUB
    blocks = rows // SUB
    copies = [
        pltpu.make_async_copy(source_tile, buffer, sems.at[n])
        for n, (source_tile, buffer) in enumerate(
            (
                (tile_weight, weight),
                (tile_coeff, coeff),
                (tile_capacity, capacity),
                (tile_conduct, conduct),
                (tile_old, before),
                (tile_forcing, forcing),
            )
        )
    ]
    for copy in copies:
        copy.start()
    even = parity[0] == 0
    pair, following = pair_edge[...], next_edge[...]
    low_edge[...] = pltpu.roll(jnp.where(even, following, pair), 1, 1) * 0.25
    high_edge[...] = pltpu.roll(jnp.where(even, pair, following), LANES - 1, 1) * 0.25
    row, lane = row_index((SUB, LANES)), lane_index((SUB, LANES))
    low_corner = (row == 0) & (lane == 0)
    high_corner = (row == SUB - 1) & (lane == LANES - 1)
    at_last, at_first = lane == LANES - 1, lane == 0
    blank = jnp.zeros((SUB, LANES), F32)

    def smooth_at(level):
        values = []
        for g in range(blocks):
            top = SUB + g * SUB
            here = padded[level, pl.ds(top, SUB), :]
            above = padded[level, pl.ds(top - 1, SUB), :]
            below = padded[level, pl.ds(top + 1, SUB), :]
            left = pltpu.roll(jnp.where(at_last, above, here), 1, 1)
            right = pltpu.roll(jnp.where(at_first, below, here), LANES - 1, 1)
            values.append((left + 2.0 * here + right) * 0.25)
        low = jnp.broadcast_to(low_edge[pl.ds(level, 1), :], (SUB, LANES))
        high = jnp.broadcast_to(high_edge[pl.ds(level, 1), :], (SUB, LANES))
        values[0] = values[0] + jnp.where(low_corner, low, blank)
        values[-1] = values[-1] + jnp.where(high_corner, high, blank)
        return values

    def old_at(level, g):
        return old[level, pl.ds(g * SUB * LANES, SUB * LANES)].reshape(SUB, LANES)

    def step(level, carried):
        conduct_u, right_n = carried
        below = smooth_at(level - 1)
        next_u, next_n = [], []
        for g in range(blocks):
            inverse = reciprocal(conduct_u[g] + below[g])
            e = right_n[g] * inverse
            offset[level - 2, pl.ds(g * SUB, SUB), :] = e
            factor[level - 2, pl.ds(g * SUB, SUB), :] = below[g] * inverse
            next_u.append(1.0 + (below[g] * conduct_u[g]) * inverse)
            next_n.append(old_at(level - 1, g) + below[g] * e)
        return next_u, next_n

    top = [old_at(levels, g) for g in range(blocks)]
    ones = [jnp.ones((SUB, LANES), F32) for _ in range(blocks)]
    conduct_u, right_n = ones, top
    for level in range(levels, 1, -1):
        conduct_u, right_n = step(level, (conduct_u, right_n))
    ground = smooth_at(0)
    for g in range(blocks):
        here = pl.ds(g * SUB, SUB)
        params[0, here, :] = old_at(0, g)
        params[1, here, :] = right_n[g]
        params[2, here, :] = conduct_u[g]
        params[3, here, :] = ground[g]
    for copy in copies:
        copy.wait()
    tiles = weight.shape[0]

    def tile_block(g, carried):
        columns = pl.ds(pl.multiple_of(g * SUB * LANES, SUB * LANES), SUB * LANES)
        here = pl.ds(pl.multiple_of(g * SUB, SUB), SUB)
        weight_sum = land_a = land_b = blank
        for t in range(tiles):
            w, c, cap, con, was, force = (
                buffer[t, columns].reshape(SUB, LANES)
                for buffer in (weight, coeff, capacity, conduct, before, forcing)
            )
            keep = cap + con
            inverse = reciprocal(keep + c)
            src = cap * was + force
            slope = c * inverse
            tile_base[t, here, :] = src * inverse
            tile_slope[t, here, :] = slope
            share = w * slope
            weight_sum = weight_sum + w
            land_a = land_a + share * src
            land_b = land_b + share * keep
        inverse = reciprocal(weight_sum)
        land[0, here, :] = land_a * inverse
        land[1, here, :] = land_b * inverse
        return carried

    lax.fori_loop(0, blocks, tile_block, 0)
    pick, lead, rest = source[...], first[...], second[...]
    halves = []
    for n in range(4):
        moved = jnp.take_along_axis(params[n], pick, axis=1)
        halves.append(jnp.concatenate([moved * lead, moved * rest], axis=0))
    packed = select_rows(place[...], jnp.concatenate(halves, axis=1))
    for n in range(4):
        field = packed[:, n * LANES : (n + 1) * LANES]
        if fast:
            for k, block in enumerate(exchange([field[g * SUB : (g + 1) * SUB] for g in range(blocks)])):
                send[k, 2 + n] = block
        else:
            send[n] = field
    if fast:
        for k in range(blocks):
            for n in range(2):
                send[k, n] = land[n, pl.ds(k * SUB, SUB), :]


def finish(
    fast,
    inbox,
    slots,
    offset,
    factor,
    params,
    land,
    tile_base,
    tile_slope,
    fetch,
    spot,
    mask,
    sea,
    column_temp,
    tile_temp,
    solved,
    warm,
    column_buffer,
    tile_buffer,
    sems,
    tile_sem,
):
    upper, rows, _ = offset.shape
    blocks = rows // SUB
    tiles = tile_base.shape[0]
    fields = []
    for n in range(2):
        if fast:
            fields.append(
                jnp.concatenate(exchange([inbox[k, n] for k in range(blocks)]), axis=0)
            )
        else:
            fields.append(inbox[n])
    windows = select_rows(fetch[...], jnp.concatenate(fields, axis=1))
    place = spot[...]
    lane, upper_half = place & (LANES - 1), place >= LANES
    is_land = mask[...] == 1
    for n, ocean in ((0, sea[...]), (1, jnp.ones((rows, LANES), F32))):
        one = windows[:rows, n * LANES : (n + 1) * LANES]
        two = windows[rows:, n * LANES : (n + 1) * LANES]
        found = jnp.where(
            upper_half,
            jnp.take_along_axis(two, lane, axis=1),
            jnp.take_along_axis(one, lane, axis=1),
        )
        solved[n] = jnp.where(is_land, found, ocean)

    def update(a, b, base, n1, w, ground, flux):
        k = ground * (1.0 + 0.5 * jnp.tanh(flux))
        total = w + k
        surface = ((base + a) * total + k * n1) * reciprocal((1.0 + b) * total + w * k)
        return k, surface, a - b * surface

    zero = jnp.zeros((SUB, LANES), F32)
    spans = [pl.ds(g * SUB, SUB) for g in range(blocks)]

    def over_columns(repeat, flux):
        fluxes = []
        for here, last in zip(spans, flux):
            k, surface, next_flux = update(
                solved[0, here, :], solved[1, here, :], *(params[n, here, :] for n in range(4)), last
            )
            column_buffer[0, here, :] = surface
            column_buffer[1, here, :] = k
            fluxes.append(next_flux)
        return fluxes

    def land_params(i):
        return [inbox[i, 2 + n] if fast else slots[n, spans[i], :] for n in range(4)]

    def over_land(repeat, flux):
        fluxes = []
        for i, (here, last) in enumerate(zip(spans, flux)):
            base, n1, w, ground = land_params(i)
            w = jnp.where(ground > 0.0, w, 1.0)
            _, surface, next_flux = update(
                land[0, here, :], land[1, here, :], base, n1, w, ground, last
            )
            warm[here, :] = surface
            fluxes.append(next_flux)
        return fluxes

    width = 2
    parts = blocks // width

    def solve_columns(part):
        chosen = spans[part * width : (part + 1) * width]
        values = []
        for here in chosen:
            surface, k = column_buffer[0, here, :], column_buffer[1, here, :]
            n1, w = params[1, here, :], params[2, here, :]
            value = (n1 + k * surface) * reciprocal(w + k)
            column_buffer[1, here, :] = value
            values.append(value)

        def substitute(level, values):
            values = [
                offset[level, here, :] + factor[level, here, :] * value
                for here, value in zip(chosen, values)
            ]
            for here, value in zip(chosen, values):
                column_buffer[level + 2, here, :] = value
            return values

        lax.fori_loop(0, upper, substitute, values, unroll=upper // 4)
        for t in range(part * width * SUB, (part + 1) * width * SUB):
            pltpu.make_async_copy(
                column_buffer.at[:, t, :],
                column_temp.at[:, pl.ds(t * LANES, LANES)],
                sems.at[part],
            ).start()

    lax.fori_loop(0, ITERS, over_columns, [zero] * blocks, unroll=2)
    early = min(2, parts)
    for part in range(early):
        solve_columns(part)
    lax.fori_loop(0, ITERS, over_land, [zero] * blocks, unroll=2)
    for i, here in enumerate(spans):
        surface = jnp.where(land_params(i)[3] > 0.0, warm[here, :], zero)
        for t in range(tiles):
            tile_buffer[t, here, :] = tile_base[t, here, :] + tile_slope[t, here, :] * surface
    for t in range(rows):
        pltpu.make_async_copy(
            tile_buffer.at[:, t, :], tile_temp.at[:, pl.ds(t * LANES, LANES)], tile_sem
        ).start()
    for part in range(early, parts):
        solve_columns(part)
    pltpu.make_async_copy(tile_buffer, tile_buffer, tile_sem).wait()
    for part in range(parts):
        span = column_buffer.at[:, pl.ds(part * width * SUB, width * SUB), :]
        pltpu.make_async_copy(span, span, sems.at[part]).wait()


def on_device(
    column_old,
    coupling,
    sea_temp,
    land_mask,
    tile_weight,
    tile_coeff,
    tile_capacity,
    tile_conduct,
    tile_old,
    tile_forcing,
):
    axes = ("lon", "lev")
    couplings, columns = coupling.shape
    levels = column_old.shape[0]
    tiles = tile_weight.shape[0]
    peers = lax.axis_size("lon")
    slot_count = columns // peers
    rows = columns // LANES
    blocks = rows // SUB
    fast = peers == SUB and rows == SUB * SUB
    devices = peers * lax.axis_size("lev")
    parity = lax.rem(lax.axis_index(axes), 2)
    pairs = [(i, i ^ 1) for i in range(devices)]
    following = [(i, (i + 1 if i % 2 else i - 1) % devices) for i in range(devices)]
    hbm, vmem, smem = pl.ANY, pltpu.VMEM, pltpu.SMEM
    full = (rows, LANES)
    mask = land_mask.reshape(full)
    table_outs = [
        VMEM(full, I32),
        VMEM(full, F32),
        VMEM(full, F32),
        VMEM((rows, 6 * rows), jnp.bfloat16),
        VMEM((2 * rows, 3 * rows), jnp.bfloat16),
        VMEM(full, I32),
    ]
    edge = (couplings, LANES)
    next_own, pair_own = chip_call(
        cut_edges,
        [VMEM(edge, F32)] * 2,
        [smem, pltpu.HBM],
        [vmem] * 2,
        [VMEM(edge, F32)] * 2 + [DMA((2,))],
        (parity.reshape(1), coupling),
        pl.CostEstimate(flops=0, bytes_accessed=16 * couplings * LANES, transcendentals=0),
        EDGE_GRANT,
    )
    next_edge = lax.ppermute(next_own, axes, following)
    pair_edge = lax.ppermute(pair_own, axes, pairs)
    padded, source, first, second, place, fetch, spot = chip_call(
        functools.partial(prepare, fast),
        [VMEM((couplings, rows + 2 * SUB, LANES), F32)] + table_outs,
        [pltpu.HBM] * 2,
        [vmem] * 7,
        [VMEM(full, I32), DMA, DMA],
        (coupling, mask),
        pl.CostEstimate(
            flops=8 * couplings * columns, bytes_accessed=8 * levels * columns, transcendentals=0
        ),
        WIDE_GRANT,
    )
    sent = (peers, 6, SUB, LANES) if fast else (4,) + full
    handed = VMEM if fast else jax.ShapeDtypeStruct
    offset, factor, params, land, tile_base, tile_slope, send = chip_call(
        functools.partial(eliminate, fast),
        [
            VMEM((levels - 2,) + full, F32),
            VMEM((levels - 2,) + full, F32),
            VMEM((4,) + full, F32),
            handed((2,) + full, F32),
            VMEM((tiles,) + full, F32),
            VMEM((tiles,) + full, F32),
            handed(sent, F32),
        ],
        [smem] + [vmem] * 8 + [pltpu.HBM] * 6,
        [vmem] * 7,
        [VMEM((couplings, LANES), F32)] * 2 + [VMEM((tiles, columns), F32)] * 6 + [DMA((6,))],
        (
            parity.reshape(1),
            padded,
            on_chip(column_old),
            pair_edge,
            next_edge,
            source,
            first,
            second,
            place,
            tile_weight,
            tile_coeff,
            tile_capacity,
            tile_conduct,
            tile_old,
            tile_forcing,
        ),
        pl.CostEstimate(
            flops=20 * levels * columns, bytes_accessed=24 * tiles * columns, transcendentals=0
        ),
        TILE_GRANT,
    )
    if fast:
        inbox = lax.all_to_all(send, "lon", split_axis=0, concat_axis=0, tiled=True)
        slots = inbox
    else:
        ranked = send.reshape(4, slot_count, peers).transpose(2, 0, 1)
        own = land.reshape(2, peers, slot_count).transpose(1, 0, 2)
        got = lax.all_to_all(
            jnp.concatenate([own, ranked], axis=1), "lon", split_axis=0, concat_axis=0, tiled=True
        )
        inbox = got[:, :2].transpose(1, 2, 0).reshape((2,) + full)
        slots = got[:, 2:].transpose(1, 0, 2).reshape((4,) + full)
    width = 2
    column_temp, tile_temp = chip_call(
        functools.partial(finish, fast),
        [
            jax.ShapeDtypeStruct(column_old.shape, F32),
            jax.ShapeDtypeStruct(tile_old.shape, F32),
        ],
        [vmem] * 12,
        [hbm, hbm],
        [
            VMEM((2,) + full, F32),
            VMEM(full, F32),
            VMEM((levels,) + full, F32),
            VMEM((tiles,) + full, F32),
            DMA((blocks // width,)),
            DMA,
        ],
        (
            inbox,
            slots,
            offset,
            factor,
            params,
            land,
            tile_base,
            tile_slope,
            fetch,
            spot,
            mask,
            sea_temp.reshape(full),
        ),
        pl.CostEstimate(
            flops=4 * levels * columns, bytes_accessed=4 * levels * columns, transcendentals=0
        ),
    )
    return column_temp, tile_temp


def solution(mesh):
    wide, flat = P(None, ("lon", "lev")), P(("lon", "lev"))
    in_specs = (wide, wide, flat, flat) + (wide,) * 6
    return jax.shard_map(
        on_device, mesh=mesh, in_specs=in_specs, out_specs=(wide, wide), check_vma=False
    )
```

```python
import functools

import jax
import jax.numpy as jnp
from jax import lax
from jax.experimental import pallas as pl
from jax.experimental.pallas import tpu as pltpu
from jax.sharding import PartitionSpec as P


ITERS = 8
LANES = 128
SUB = 8
GRANT = 16 * 1024 * 1024
WIDE_GRANT = 55 * 1024 * 1024
EDGE_GRANT = 62 * 1024 * 1024
TILE_GRANT = 48 * 1024 * 1024
F32 = jnp.float32
I32 = jnp.int32
VMEM = pltpu.VMEM
DMA = pltpu.SemaphoreType.DMA


def on_chip(array):
    return pltpu.with_memory_space_constraint(array, pltpu.VMEM)


def chip_call(kernel, outs, in_spaces, out_spaces, scratch, args, cost, grant=GRANT):
    results = pl.pallas_call(
        kernel,
        out_shape=outs,
        in_specs=[pl.BlockSpec(memory_space=space) for space in in_spaces],
        out_specs=[pl.BlockSpec(memory_space=space) for space in out_spaces],
        scratch_shapes=scratch,
        cost_estimate=cost,
        compiler_params=pltpu.CompilerParams(vmem_limit_bytes=grant),
    )(*args)
    return [
        result if isinstance(out, jax.ShapeDtypeStruct) else on_chip(result)
        for result, out in zip(results, outs)
    ]


def lane_index(shape):
    return lax.broadcasted_iota(I32, shape, len(shape) - 1)


def row_index(shape):
    return lax.broadcasted_iota(I32, shape, len(shape) - 2)


def reciprocal(x):
    return 1.0 / x


def one_hot(condition):
    return jnp.where(condition, jnp.ones((), F32), jnp.zeros((), F32))


def spread(values):
    high = values.astype(jnp.bfloat16)
    rest = values - high.astype(F32)
    middle = rest.astype(jnp.bfloat16)
    low = (rest - middle.astype(F32)).astype(jnp.bfloat16)
    return jnp.concatenate([high, middle, low], axis=0)


def select_rows(chooser, values):
    return jnp.dot(chooser, spread(values), preferred_element_type=F32)


def count_dot(a, b):
    return jnp.dot(
        a.astype(jnp.bfloat16), b.astype(jnp.bfloat16), preferred_element_type=F32
    )


def lane_of(position, fast):
    return (position & 7) * 16 + (position >> 3) if fast else position


def position_of(lane, fast):
    return (lane & 15) * 8 + (lane >> 4) if fast else lane


def rank_row_of(row, fast):
    return (row & 7) * 8 + (row >> 3) if fast else row


def exchange(blocks):
    group = lane_index((SUB, LANES)) >> 4
    step = 1
    while step < SUB:
        high = (group & step) != 0
        done = list(blocks)
        for low in range(SUB):
            if low & step:
                continue
            a, b = blocks[low], blocks[low + step]
            done[low] = jnp.where(high, pltpu.roll(b, 16 * step, 1), a)
            done[low + step] = jnp.where(high, b, pltpu.roll(a, LANES - 16 * step, 1))
        blocks = done
        step *= 2
    return blocks


def build_tables(fast, mask, source_ref, first_ref, second_ref, place_ref, fetch_ref, spot_ref):
    rows = mask.shape[0]
    shape = (rows, LANES)
    land = mask.astype(F32)
    upper = one_hot(row_index((LANES, LANES)) <= lane_index((LANES, LANES)))
    running = count_dot(land, upper)
    totals = count_dot(land, jnp.ones((LANES, LANES), F32))
    before = one_hot(lane_index((rows, rows)) < row_index((rows, rows)))
    base = count_dot(before, totals).astype(I32)
    totals = totals.astype(I32)
    running = running.astype(I32)
    start = base & (LANES - 1)
    position = position_of(lane_index(shape), fast)
    ordinal = (position - start) & (LANES - 1)
    source = jnp.zeros(shape, I32)
    step = LANES // 2
    while step:
        reached = jnp.take_along_axis(running, source + (step - 1), axis=1)
        source = jnp.where(reached <= ordinal, source + step, source)
        step //= 2
    source_ref[...] = source
    valid = ordinal < totals
    first_ref[...] = one_hot(valid & (position >= start))
    second_ref[...] = one_hot(valid & (position < start))
    row_totals = lax.dot_general(
        jnp.ones((SUB, LANES), jnp.bfloat16),
        land.astype(jnp.bfloat16),
        (((1,), (1,)), ((), ())),
        preferred_element_type=F32,
    )
    earlier = one_hot(row_index((rows, rows)) < lane_index((rows, rows)))
    base_row = count_dot(row_totals, earlier).astype(I32)[:1]
    lead_row = jnp.broadcast_to(base_row >> 7, (rows, rows))
    wanted = rank_row_of(row_index((rows, rows)), fast)
    place_ref[...] = jnp.concatenate(
        [one_hot(lead_row == wanted), one_hot(lead_row + 1 == wanted)] * 3, axis=1
    ).astype(jnp.bfloat16)
    lead = (base >> 7)[:, :rows] if rows <= LANES else base[:, :1] >> 7
    held = rank_row_of(lane_index((rows, rows)), fast)
    chooser = jnp.concatenate([one_hot(lead == held), one_hot(lead + 1 == held)], axis=0)
    fetch_ref[...] = jnp.concatenate([chooser] * 3, axis=1).astype(jnp.bfloat16)
    spot = start + running - 1
    spot_ref[...] = lane_of(spot & (LANES - 1), fast) + (spot & LANES)


def cut_edges(parity, coupling, next_edge, pair_edge, low, high, sems):
    columns = coupling.shape[1]
    copies = [
        pltpu.make_async_copy(coupling.at[:, pl.ds(0, LANES)], low, sems.at[0]),
        pltpu.make_async_copy(coupling.at[:, pl.ds(columns - LANES, LANES)], high, sems.at[1]),
    ]
    for copy in copies:
        copy.start()
    for copy in copies:
        copy.wait()
    even = parity[0] == 0
    next_edge[...] = jnp.where(even, low[...], high[...])
    pair_edge[...] = jnp.where(even, high[...], low[...])


def prepare(
    fast, coupling, mask, padded, source, first, second, place, fetch, spot, held, sem, mask_sem
):
    levels, height, _ = padded.shape
    rows = height - 2 * SUB
    mask_copy = pltpu.make_async_copy(mask, held, mask_sem)
    mask_copy.start()
    for t in range(rows):
        pltpu.make_async_copy(
            coupling.at[:, pl.ds(t * LANES, LANES)], padded.at[:, SUB + t, :], sem
        ).start()
    blank = jnp.zeros((SUB, LANES), F32)

    def clear(level, carried):
        padded[level, pl.ds(0, SUB), :] = blank
        padded[level, pl.ds(SUB + rows, SUB), :] = blank
        return carried

    lax.fori_loop(0, levels, clear, 0, unroll=3)
    mask_copy.wait()
    build_tables(fast, held[...], source, first, second, place, fetch, spot)
    inner = padded.at[:, pl.ds(SUB, rows), :]
    pltpu.make_async_copy(inner, inner, sem).wait()


def eliminate(
    fast,
    parity,
    padded,
    old,
    pair_edge,
    next_edge,
    source,
    first,
    second,
    place,
    tile_weight,
    tile_coeff,
    tile_capacity,
    tile_conduct,
    tile_old,
    tile_forcing,
    offset,
    factor,
    params,
    land,
    tile_base,
    tile_slope,
    send,
    low_edge,
    high_edge,
    weight,
    coeff,
    capacity,
    conduct,
    before,
    forcing,
    sems,
):
    levels, height, _ = padded.shape
    rows = height - 2 * SUB
    blocks = rows // SUB
    copies = [
        pltpu.make_async_copy(source_tile, buffer, sems.at[n])
        for n, (source_tile, buffer) in enumerate(
            (
                (tile_weight, weight),
                (tile_coeff, coeff),
                (tile_capacity, capacity),
                (tile_conduct, conduct),
                (tile_old, before),
                (tile_forcing, forcing),
            )
        )
    ]
    for copy in copies:
        copy.start()
    even = parity[0] == 0
    pair, following = pair_edge[...], next_edge[...]
    low_edge[...] = pltpu.roll(jnp.where(even, following, pair), 1, 1) * 0.25
    high_edge[...] = pltpu.roll(jnp.where(even, pair, following), LANES - 1, 1) * 0.25
    row, lane = row_index((SUB, LANES)), lane_index((SUB, LANES))
    low_corner = (row == 0) & (lane == 0)
    high_corner = (row == SUB - 1) & (lane == LANES - 1)
    at_last, at_first = lane == LANES - 1, lane == 0
    blank = jnp.zeros((SUB, LANES), F32)

    def smooth_at(level):
        values = []
        for g in range(blocks):
            top = SUB + g * SUB
            here = padded[level, pl.ds(top, SUB), :]
            above = padded[level, pl.ds(top - 1, SUB), :]
            below = padded[level, pl.ds(top + 1, SUB), :]
            left = pltpu.roll(jnp.where(at_last, above, here), 1, 1)
            right = pltpu.roll(jnp.where(at_first, below, here), LANES - 1, 1)
            values.append((left + right) * 0.25 + here * 0.5)
        low = jnp.broadcast_to(low_edge[pl.ds(level, 1), :], (SUB, LANES))
        high = jnp.broadcast_to(high_edge[pl.ds(level, 1), :], (SUB, LANES))
        values[0] = values[0] + jnp.where(low_corner, low, blank)
        values[-1] = values[-1] + jnp.where(high_corner, high, blank)
        return values

    def old_at(level, g):
        return old[level, pl.ds(g * SUB * LANES, SUB * LANES)].reshape(SUB, LANES)

    def step(level, carried):
        conduct_u, right_n = carried
        below = smooth_at(level - 1)
        next_u, next_n = [], []
        for g in range(blocks):
            inverse = reciprocal(conduct_u[g] + below[g])
            e = right_n[g] * inverse
            offset[level - 2, pl.ds(g * SUB, SUB), :] = e
            f = below[g] * inverse
            factor[level - 2, pl.ds(g * SUB, SUB), :] = f
            next_u.append(1.0 + f * conduct_u[g])
            next_n.append(old_at(level - 1, g) + f * right_n[g])
        return next_u, next_n

    top = [old_at(levels, g) for g in range(blocks)]
    ones = [jnp.ones((SUB, LANES), F32) for _ in range(blocks)]
    conduct_u, right_n = ones, top
    for level in range(levels, 1, -1):
        conduct_u, right_n = step(level, (conduct_u, right_n))
    ground = smooth_at(0)
    for g in range(blocks):
        here = pl.ds(g * SUB, SUB)
        params[0, here, :] = old_at(0, g)
        params[1, here, :] = right_n[g]
        params[2, here, :] = conduct_u[g]
        params[3, here, :] = ground[g]
    for copy in copies:
        copy.wait()
    tiles = weight.shape[0]

    def tile_block(g, carried):
        columns = pl.ds(pl.multiple_of(g * SUB * LANES, SUB * LANES), SUB * LANES)
        here = pl.ds(pl.multiple_of(g * SUB, SUB), SUB)
        weight_sum = land_a = land_b = blank
        for t in range(tiles):
            w, c, cap, con, was, force = (
                buffer[t, columns].reshape(SUB, LANES)
                for buffer in (weight, coeff, capacity, conduct, before, forcing)
            )
            keep = cap + con
            inverse = reciprocal(keep + c)
            src = cap * was + force
            slope = c * inverse
            tile_base[t, here, :] = src * inverse
            tile_slope[t, here, :] = slope
            share = w * slope
            weight_sum = weight_sum + w
            land_a = land_a + share * src
            land_b = land_b + share * keep
        inverse = reciprocal(weight_sum)
        land[0, here, :] = land_a * inverse
        land[1, here, :] = land_b * inverse
        return carried

    lax.fori_loop(0, blocks, tile_block, 0, unroll=True)
    pick, lead, rest = source[...], first[...], second[...]
    halves = []
    for n in range(4):
        moved = jnp.take_along_axis(params[n], pick, axis=1)
        halves.append(jnp.concatenate([moved * lead, moved * rest], axis=0))
    packed = select_rows(place[...], jnp.concatenate(halves, axis=1))
    for n in range(4):
        field = packed[:, n * LANES : (n + 1) * LANES]
        if fast:
            for k, block in enumerate(exchange([field[g * SUB : (g + 1) * SUB] for g in range(blocks)])):
                send[k, 2 + n] = block
        else:
            send[n] = field
    if fast:
        for k in range(blocks):
            for n in range(2):
                send[k, n] = land[n, pl.ds(k * SUB, SUB), :]


def finish(
    fast,
    inbox,
    slots,
    offset,
    factor,
    params,
    land,
    tile_base,
    tile_slope,
    fetch,
    spot,
    mask,
    sea,
    column_temp,
    tile_temp,
    solved,
    warm,
    column_buffer,
    tile_buffer,
    sems,
    tile_sem,
):
    upper, rows, _ = offset.shape
    blocks = rows // SUB
    tiles = tile_base.shape[0]
    fields = []
    for n in range(2):
        if fast:
            fields.append(
                jnp.concatenate(exchange([inbox[k, n] for k in range(blocks)]), axis=0)
            )
        else:
            fields.append(inbox[n])
    windows = select_rows(fetch[...], jnp.concatenate(fields, axis=1))
    place = spot[...]
    lane, upper_half = place & (LANES - 1), place >= LANES
    is_land = mask[...] == 1
    for n, ocean in ((0, sea[...]), (1, jnp.ones((rows, LANES), F32))):
        one = windows[:rows, n * LANES : (n + 1) * LANES]
        two = windows[rows:, n * LANES : (n + 1) * LANES]
        found = jnp.where(
            upper_half,
            jnp.take_along_axis(two, lane, axis=1),
            jnp.take_along_axis(one, lane, axis=1),
        )
        solved[n] = jnp.where(is_land, found, ocean)

    def update(a, b, base, n1, w, ground, flux):
        k = ground * (1.0 + 0.5 * jnp.tanh(flux))
        total = w + k
        surface = ((base + a) * total + k * n1) * reciprocal((1.0 + b) * total + w * k)
        return k, surface, a - b * surface

    zero = jnp.zeros((SUB, LANES), F32)
    spans = [pl.ds(g * SUB, SUB) for g in range(blocks)]

    def over_columns(repeat, flux):
        fluxes = []
        for here, last in zip(spans, flux):
            k, surface, next_flux = update(
                solved[0, here, :], solved[1, here, :], *(params[n, here, :] for n in range(4)), last
            )
            column_buffer[0, here, :] = surface
            column_buffer[1, here, :] = k
            fluxes.append(next_flux)
        return fluxes

    def land_params(i):
        return [inbox[i, 2 + n] if fast else slots[n, spans[i], :] for n in range(4)]

    def over_land(repeat, flux):
        fluxes = []
        for i, (here, last) in enumerate(zip(spans, flux)):
            base, n1, w, ground = land_params(i)
            w = jnp.where(ground > 0.0, w, 1.0)
            _, surface, next_flux = update(
                land[0, here, :], land[1, here, :], base, n1, w, ground, last
            )
            warm[here, :] = surface
            fluxes.append(next_flux)
        return fluxes

    width = 2
    parts = blocks // width

    def solve_columns(part):
        chosen = spans[part * width : (part + 1) * width]
        values = []
        for here in chosen:
            surface, k = column_buffer[0, here, :], column_buffer[1, here, :]
            n1, w = params[1, here, :], params[2, here, :]
            value = (n1 + k * surface) * reciprocal(w + k)
            column_buffer[1, here, :] = value
            values.append(value)

        def substitute(level, values):
            values = [
                offset[level, here, :] + factor[level, here, :] * value
                for here, value in zip(chosen, values)
            ]
            for here, value in zip(chosen, values):
                column_buffer[level + 2, here, :] = value
            return values

        lax.fori_loop(0, upper, substitute, values, unroll=upper // 4)
        for t in range(part * width * SUB, (part + 1) * width * SUB):
            pltpu.make_async_copy(
                column_buffer.at[:, t, :],
                column_temp.at[:, pl.ds(t * LANES, LANES)],
                sems.at[part],
            ).start()

    lax.fori_loop(0, ITERS, over_columns, [zero] * blocks, unroll=2)
    early = min(2, parts)
    for part in range(early):
        solve_columns(part)
    lax.fori_loop(0, ITERS, over_land, [zero] * blocks, unroll=2)
    for i, here in enumerate(spans):
        surface = jnp.where(land_params(i)[3] > 0.0, warm[here, :], zero)
        for t in range(tiles):
            tile_buffer[t, here, :] = tile_base[t, here, :] + tile_slope[t, here, :] * surface
    for t in range(rows):
        pltpu.make_async_copy(
            tile_buffer.at[:, t, :], tile_temp.at[:, pl.ds(t * LANES, LANES)], tile_sem
        ).start()
    for part in range(early, parts):
        solve_columns(part)
    pltpu.make_async_copy(tile_buffer, tile_buffer, tile_sem).wait()
    for part in range(parts):
        span = column_buffer.at[:, pl.ds(part * width * SUB, width * SUB), :]
        pltpu.make_async_copy(span, span, sems.at[part]).wait()


def on_device(
    column_old,
    coupling,
    sea_temp,
    land_mask,
    tile_weight,
    tile_coeff,
    tile_capacity,
    tile_conduct,
    tile_old,
    tile_forcing,
):
    axes = ("lon", "lev")
    couplings, columns = coupling.shape
    levels = column_old.shape[0]
    tiles = tile_weight.shape[0]
    peers = lax.axis_size("lon")
    slot_count = columns // peers
    rows = columns // LANES
    blocks = rows // SUB
    fast = peers == SUB and rows == SUB * SUB
    devices = peers * lax.axis_size("lev")
    parity = lax.rem(lax.axis_index(axes), 2)
    pairs = [(i, i ^ 1) for i in range(devices)]
    following = [(i, (i + 1 if i % 2 else i - 1) % devices) for i in range(devices)]
    hbm, vmem, smem = pl.ANY, pltpu.VMEM, pltpu.SMEM
    full = (rows, LANES)
    mask = land_mask.reshape(full)
    table_outs = [
        VMEM(full, I32),
        VMEM(full, F32),
        VMEM(full, F32),
        VMEM((rows, 6 * rows), jnp.bfloat16),
        VMEM((2 * rows, 3 * rows), jnp.bfloat16),
        VMEM(full, I32),
    ]
    edge = (couplings, LANES)
    next_own, pair_own = chip_call(
        cut_edges,
        [VMEM(edge, F32)] * 2,
        [smem, pltpu.HBM],
        [vmem] * 2,
        [VMEM(edge, F32)] * 2 + [DMA((2,))],
        (parity.reshape(1), coupling),
        pl.CostEstimate(flops=0, bytes_accessed=16 * couplings * LANES, transcendentals=0),
        EDGE_GRANT,
    )
    next_edge = lax.ppermute(next_own, axes, following)
    pair_edge = lax.ppermute(pair_own, axes, pairs)
    padded, source, first, second, place, fetch, spot = chip_call(
        functools.partial(prepare, fast),
        [VMEM((couplings, rows + 2 * SUB, LANES), F32)] + table_outs,
        [pltpu.HBM] * 2,
        [vmem] * 7,
        [VMEM(full, I32), DMA, DMA],
        (coupling, mask),
        pl.CostEstimate(
            flops=8 * couplings * columns, bytes_accessed=8 * levels * columns, transcendentals=0
        ),
        WIDE_GRANT,
    )
    sent = (peers, 6, SUB, LANES) if fast else (4,) + full
    handed = VMEM if fast else jax.ShapeDtypeStruct
    offset, factor, params, land, tile_base, tile_slope, send = chip_call(
        functools.partial(eliminate, fast),
        [
            VMEM((levels - 2,) + full, F32),
            VMEM((levels - 2,) + full, F32),
            VMEM((4,) + full, F32),
            handed((2,) + full, F32),
            VMEM((tiles,) + full, F32),
            VMEM((tiles,) + full, F32),
            handed(sent, F32),
        ],
        [smem] + [vmem] * 8 + [pltpu.HBM] * 6,
        [vmem] * 7,
        [VMEM((couplings, LANES), F32)] * 2 + [VMEM((tiles, columns), F32)] * 6 + [DMA((6,))],
        (
            parity.reshape(1),
            padded,
            on_chip(column_old),
            pair_edge,
            next_edge,
            source,
            first,
            second,
            place,
            tile_weight,
            tile_coeff,
            tile_capacity,
            tile_conduct,
            tile_old,
            tile_forcing,
        ),
        pl.CostEstimate(
            flops=20 * levels * columns, bytes_accessed=24 * tiles * columns, transcendentals=0
        ),
        TILE_GRANT,
    )
    if fast:
        inbox = lax.all_to_all(send, "lon", split_axis=0, concat_axis=0, tiled=True)
        slots = inbox
    else:
        ranked = send.reshape(4, slot_count, peers).transpose(2, 0, 1)
        own = land.reshape(2, peers, slot_count).transpose(1, 0, 2)
        got = lax.all_to_all(
            jnp.concatenate([own, ranked], axis=1), "lon", split_axis=0, concat_axis=0, tiled=True
        )
        inbox = got[:, :2].transpose(1, 2, 0).reshape((2,) + full)
        slots = got[:, 2:].transpose(1, 0, 2).reshape((4,) + full)
    width = 2
    column_temp, tile_temp = chip_call(
        functools.partial(finish, fast),
        [
            jax.ShapeDtypeStruct(column_old.shape, F32),
            jax.ShapeDtypeStruct(tile_old.shape, F32),
        ],
        [vmem] * 12,
        [hbm, hbm],
        [
            VMEM((2,) + full, F32),
            VMEM(full, F32),
            VMEM((levels,) + full, F32),
            VMEM((tiles,) + full, F32),
            DMA((blocks // width,)),
            DMA,
        ],
        (
            inbox,
            slots,
            offset,
            factor,
            params,
            land,
            tile_base,
            tile_slope,
            fetch,
            spot,
            mask,
            sea_temp.reshape(full),
        ),
        pl.CostEstimate(
            flops=4 * levels * columns, bytes_accessed=4 * levels * columns, transcendentals=0
        ),
    )
    return column_temp, tile_temp


def solution(mesh):
    wide, flat = P(None, ("lon", "lev")), P(("lon", "lev"))
    in_specs = (wide, wide, flat, flat) + (wide,) * 6
    return jax.shard_map(
        on_device, mesh=mesh, in_specs=in_specs, out_specs=(wide, wide), check_vma=False
    )
```

```python
import functools

import jax
import jax.numpy as jnp
from jax import lax
from jax.experimental import pallas as pl
from jax.experimental.pallas import tpu as pltpu
from jax.sharding import PartitionSpec as P


ITERS = 8
LANES = 128
SUB = 8
GRANT = 16 * 1024 * 1024
WIDE_GRANT = 55 * 1024 * 1024
EDGE_GRANT = 62 * 1024 * 1024
TILE_GRANT = 48 * 1024 * 1024
F32 = jnp.float32
I32 = jnp.int32
VMEM = pltpu.VMEM
DMA = pltpu.SemaphoreType.DMA


def on_chip(array):
    return pltpu.with_memory_space_constraint(array, pltpu.VMEM)


def chip_call(kernel, outs, in_spaces, out_spaces, scratch, args, cost, grant=GRANT):
    results = pl.pallas_call(
        kernel,
        out_shape=outs,
        in_specs=[pl.BlockSpec(memory_space=space) for space in in_spaces],
        out_specs=[pl.BlockSpec(memory_space=space) for space in out_spaces],
        scratch_shapes=scratch,
        cost_estimate=cost,
        compiler_params=pltpu.CompilerParams(vmem_limit_bytes=grant),
    )(*args)
    return [
        result if isinstance(out, jax.ShapeDtypeStruct) else on_chip(result)
        for result, out in zip(results, outs)
    ]


def lane_index(shape):
    return lax.broadcasted_iota(I32, shape, len(shape) - 1)


def row_index(shape):
    return lax.broadcasted_iota(I32, shape, len(shape) - 2)


def reciprocal(x):
    return 1.0 / x


def one_hot(condition):
    return jnp.where(condition, jnp.ones((), F32), jnp.zeros((), F32))


def spread(values):
    high = values.astype(jnp.bfloat16)
    rest = values - high.astype(F32)
    middle = rest.astype(jnp.bfloat16)
    low = (rest - middle.astype(F32)).astype(jnp.bfloat16)
    return jnp.concatenate([high, middle, low], axis=0)


def select_rows(chooser, values):
    return jnp.dot(chooser, spread(values), preferred_element_type=F32)


def count_dot(a, b):
    return jnp.dot(
        a.astype(jnp.bfloat16), b.astype(jnp.bfloat16), preferred_element_type=F32
    )


def lane_of(position, fast):
    return (position & 7) * 16 + (position >> 3) if fast else position


def position_of(lane, fast):
    return (lane & 15) * 8 + (lane >> 4) if fast else lane


def rank_row_of(row, fast):
    return (row & 7) * 8 + (row >> 3) if fast else row


def exchange(blocks):
    group = lane_index((SUB, LANES)) >> 4
    step = 1
    while step < SUB:
        high = (group & step) != 0
        done = list(blocks)
        for low in range(SUB):
            if low & step:
                continue
            a, b = blocks[low], blocks[low + step]
            done[low] = jnp.where(high, pltpu.roll(b, 16 * step, 1), a)
            done[low + step] = jnp.where(high, b, pltpu.roll(a, LANES - 16 * step, 1))
        blocks = done
        step *= 2
    return blocks


def build_tables(fast, mask, source_ref, first_ref, second_ref, place_ref, fetch_ref, spot_ref):
    rows = mask.shape[0]
    shape = (rows, LANES)
    land = mask.astype(F32)
    upper = one_hot(row_index((LANES, LANES)) <= lane_index((LANES, LANES)))
    running = count_dot(land, upper)
    totals = count_dot(land, jnp.ones((LANES, LANES), F32))
    before = one_hot(lane_index((rows, rows)) < row_index((rows, rows)))
    base = count_dot(before, totals).astype(I32)
    totals = totals.astype(I32)
    running = running.astype(I32)
    start = base & (LANES - 1)
    position = position_of(lane_index(shape), fast)
    ordinal = (position - start) & (LANES - 1)
    source = jnp.zeros(shape, I32)
    step = LANES // 2
    while step:
        reached = jnp.take_along_axis(running, source + (step - 1), axis=1)
        source = jnp.where(reached <= ordinal, source + step, source)
        step //= 2
    source_ref[...] = source
    valid = ordinal < totals
    first_ref[...] = one_hot(valid & (position >= start))
    second_ref[...] = one_hot(valid & (position < start))
    row_totals = lax.dot_general(
        jnp.ones((SUB, LANES), jnp.bfloat16),
        land.astype(jnp.bfloat16),
        (((1,), (1,)), ((), ())),
        preferred_element_type=F32,
    )
    earlier = one_hot(row_index((rows, rows)) < lane_index((rows, rows)))
    base_row = count_dot(row_totals, earlier).astype(I32)[:1]
    lead_row = jnp.broadcast_to(base_row >> 7, (rows, rows))
    wanted = rank_row_of(row_index((rows, rows)), fast)
    place_ref[...] = jnp.concatenate(
        [one_hot(lead_row == wanted), one_hot(lead_row + 1 == wanted)] * 3, axis=1
    ).astype(jnp.bfloat16)
    lead = (base >> 7)[:, :rows] if rows <= LANES else base[:, :1] >> 7
    held = rank_row_of(lane_index((rows, rows)), fast)
    chooser = jnp.concatenate([one_hot(lead == held), one_hot(lead + 1 == held)], axis=0)
    fetch_ref[...] = jnp.concatenate([chooser] * 3, axis=1).astype(jnp.bfloat16)
    spot = start + running - 1
    spot_ref[...] = lane_of(spot & (LANES - 1), fast) + (spot & LANES)


def is_even():
    return lax.rem(lax.axis_index("lon") * lax.axis_size("lev") + lax.axis_index("lev"), 2) == 0


def cut_edges(coupling, next_edge, pair_edge, sems):
    last = coupling.shape[1] - LANES
    even = is_even()
    near = pl.multiple_of(jnp.where(even, last, 0), LANES)
    far = pl.multiple_of(jnp.where(even, 0, last), LANES)
    copies = [
        pltpu.make_async_copy(coupling.at[:, pl.ds(far, LANES)], next_edge, sems.at[0]),
        pltpu.make_async_copy(coupling.at[:, pl.ds(near, LANES)], pair_edge, sems.at[1]),
    ]
    for copy in copies:
        copy.start()
    for copy in copies:
        copy.wait()


def prepare(
    fast, coupling, mask, padded, source, first, second, place, fetch, spot, held, sem, mask_sem
):
    levels, height, _ = padded.shape
    rows = height - 2 * SUB
    mask_copy = pltpu.make_async_copy(mask, held, mask_sem)
    mask_copy.start()
    for t in range(rows):
        pltpu.make_async_copy(
            coupling.at[:, pl.ds(t * LANES, LANES)], padded.at[:, SUB + t, :], sem
        ).start()
    blank = jnp.zeros((SUB, LANES), F32)

    def clear(level, carried):
        padded[level, pl.ds(0, SUB), :] = blank
        padded[level, pl.ds(SUB + rows, SUB), :] = blank
        return carried

    lax.fori_loop(0, levels, clear, 0, unroll=3)
    mask_copy.wait()
    build_tables(fast, held[...], source, first, second, place, fetch, spot)
    inner = padded.at[:, pl.ds(SUB, rows), :]
    pltpu.make_async_copy(inner, inner, sem).wait()


def eliminate(
    fast,
    padded,
    old,
    pair_edge,
    next_edge,
    source,
    first,
    second,
    place,
    tile_weight,
    tile_coeff,
    tile_capacity,
    tile_conduct,
    tile_old,
    tile_forcing,
    offset,
    factor,
    params,
    land,
    tile_base,
    tile_slope,
    send,
    low_edge,
    high_edge,
    weight,
    coeff,
    capacity,
    conduct,
    before,
    forcing,
    sems,
):
    levels, height, _ = padded.shape
    rows = height - 2 * SUB
    blocks = rows // SUB
    copies = [
        pltpu.make_async_copy(source_tile, buffer, sems.at[n])
        for n, (source_tile, buffer) in enumerate(
            (
                (tile_weight, weight),
                (tile_coeff, coeff),
                (tile_capacity, capacity),
                (tile_conduct, conduct),
                (tile_old, before),
                (tile_forcing, forcing),
            )
        )
    ]
    for copy in copies:
        copy.start()
    even = is_even()

    def turn(rows_here):
        pair, following = pair_edge[rows_here, :], next_edge[rows_here, :]
        low = jnp.where(even, following, pair)
        high = jnp.where(even, pair, following)
        low_edge[rows_here, :] = pltpu.roll(low, 1, 1) * 0.25
        high_edge[rows_here, :] = pltpu.roll(high, LANES - 1, 1) * 0.25

    half = levels // (2 * SUB) * SUB

    def turn_half(index, carried):
        turn(pl.ds(pl.multiple_of(index * half, SUB), half))
        return carried

    lax.fori_loop(0, 2, turn_half, 0)
    if levels > 2 * half:
        turn(pl.ds(2 * half, levels - 2 * half))
    row, lane = row_index((SUB, LANES)), lane_index((SUB, LANES))
    low_corner = (row == 0) & (lane == 0)
    high_corner = (row == SUB - 1) & (lane == LANES - 1)
    at_last, at_first = lane == LANES - 1, lane == 0
    blank = jnp.zeros((SUB, LANES), F32)

    def smooth_at(level):
        values = []
        for g in range(blocks):
            top = SUB + g * SUB
            here = padded[level, pl.ds(top, SUB), :]
            above = padded[level, pl.ds(top - 1, SUB), :]
            below = padded[level, pl.ds(top + 1, SUB), :]
            left = pltpu.roll(jnp.where(at_last, above, here), 1, 1)
            right = pltpu.roll(jnp.where(at_first, below, here), LANES - 1, 1)
            values.append((left + right) * 0.25 + here * 0.5)
        low = jnp.broadcast_to(low_edge[pl.ds(level, 1), :], (SUB, LANES))
        high = jnp.broadcast_to(high_edge[pl.ds(level, 1), :], (SUB, LANES))
        values[0] = values[0] + jnp.where(low_corner, low, blank)
        values[-1] = values[-1] + jnp.where(high_corner, high, blank)
        return values

    def old_at(level, g):
        return old[level, pl.ds(g * SUB * LANES, SUB * LANES)].reshape(SUB, LANES)

    def step(level, carried):
        conduct_u, right_n = carried
        below = smooth_at(level - 1)
        next_u, next_n = [], []
        for g in range(blocks):
            inverse = reciprocal(conduct_u[g] + below[g])
            e = right_n[g] * inverse
            offset[level - 2, pl.ds(g * SUB, SUB), :] = e
            f = below[g] * inverse
            factor[level - 2, pl.ds(g * SUB, SUB), :] = f
            next_u.append(1.0 + f * conduct_u[g])
            next_n.append(old_at(level - 1, g) + f * right_n[g])
        return next_u, next_n

    top = [old_at(levels, g) for g in range(blocks)]
    ones = [jnp.ones((SUB, LANES), F32) for _ in range(blocks)]
    conduct_u, right_n = ones, top
    for level in range(levels, 1, -1):
        conduct_u, right_n = step(level, (conduct_u, right_n))
    ground = smooth_at(0)
    for g in range(blocks):
        here = pl.ds(g * SUB, SUB)
        params[0, here, :] = old_at(0, g)
        params[1, here, :] = right_n[g]
        params[2, here, :] = conduct_u[g]
        params[3, here, :] = ground[g]
    pick, lead, rest = source[...], first[...], second[...]
    halves = []
    for n in range(4):
        moved = jnp.take_along_axis(params[n], pick, axis=1)
        halves.append(jnp.concatenate([moved * lead, moved * rest], axis=0))
    packed = select_rows(place[...], jnp.concatenate(halves, axis=1))
    for n in range(4):
        field = packed[:, n * LANES : (n + 1) * LANES]
        if fast:
            for k, block in enumerate(exchange([field[g * SUB : (g + 1) * SUB] for g in range(blocks)])):
                send[k, 2 + n] = block
        else:
            send[n] = field
    for copy in copies:
        copy.wait()
    tiles = weight.shape[0]

    def tile_block(g, carried):
        columns = pl.ds(pl.multiple_of(g * SUB * LANES, SUB * LANES), SUB * LANES)
        here = pl.ds(pl.multiple_of(g * SUB, SUB), SUB)
        weight_sum = land_a = land_b = blank
        for t in range(tiles):
            w, c, cap, con, was, force = (
                buffer[t, columns].reshape(SUB, LANES)
                for buffer in (weight, coeff, capacity, conduct, before, forcing)
            )
            keep = cap + con
            inverse = reciprocal(keep + c)
            src = cap * was + force
            slope = c * inverse
            tile_base[t, here, :] = src * inverse
            tile_slope[t, here, :] = slope
            share = w * slope
            weight_sum = weight_sum + w
            land_a = land_a + share * src
            land_b = land_b + share * keep
        inverse = reciprocal(weight_sum)
        land[0, here, :] = land_a * inverse
        land[1, here, :] = land_b * inverse
        return carried

    lax.fori_loop(0, blocks, tile_block, 0, unroll=True)
    if fast:
        for k in range(blocks):
            for n in range(2):
                send[k, n] = land[n, pl.ds(k * SUB, SUB), :]


def finish(
    fast,
    inbox,
    slots,
    offset,
    factor,
    params,
    land,
    tile_base,
    tile_slope,
    fetch,
    spot,
    mask,
    sea,
    column_temp,
    tile_temp,
    solved,
    warm,
    column_buffer,
    tile_buffer,
    sems,
    tile_sem,
):
    upper, rows, _ = offset.shape
    blocks = rows // SUB
    tiles = tile_base.shape[0]
    fields = []
    for n in range(2):
        if fast:
            fields.append(
                jnp.concatenate(exchange([inbox[k, n] for k in range(blocks)]), axis=0)
            )
        else:
            fields.append(inbox[n])
    windows = select_rows(fetch[...], jnp.concatenate(fields, axis=1))
    place = spot[...]
    lane, upper_half = place & (LANES - 1), place >= LANES
    is_land = mask[...] == 1
    for n, ocean in ((0, sea[...]), (1, jnp.ones((rows, LANES), F32))):
        one = windows[:rows, n * LANES : (n + 1) * LANES]
        two = windows[rows:, n * LANES : (n + 1) * LANES]
        found = jnp.where(
            upper_half,
            jnp.take_along_axis(two, lane, axis=1),
            jnp.take_along_axis(one, lane, axis=1),
        )
        solved[n] = jnp.where(is_land, found, ocean)

    def update(a, b, base, n1, w, ground, flux):
        k = ground * (1.0 + 0.5 * jnp.tanh(flux))
        total = w + k
        surface = ((base + a) * total + k * n1) * reciprocal((1.0 + b) * total + w * k)
        return k, surface, a - b * surface

    zero = jnp.zeros((SUB, LANES), F32)
    spans = [pl.ds(g * SUB, SUB) for g in range(blocks)]

    def over_columns(repeat, flux):
        fluxes = []
        for here, last in zip(spans, flux):
            k, surface, next_flux = update(
                solved[0, here, :], solved[1, here, :], *(params[n, here, :] for n in range(4)), last
            )
            column_buffer[0, here, :] = surface
            column_buffer[1, here, :] = k
            fluxes.append(next_flux)
        return fluxes

    def land_params(i):
        return [inbox[i, 2 + n] if fast else slots[n, spans[i], :] for n in range(4)]

    def over_land(repeat, flux):
        fluxes = []
        for i, (here, last) in enumerate(zip(spans, flux)):
            base, n1, w, ground = land_params(i)
            w = jnp.where(ground > 0.0, w, 1.0)
            _, surface, next_flux = update(
                land[0, here, :], land[1, here, :], base, n1, w, ground, last
            )
            warm[here, :] = surface
            fluxes.append(next_flux)
        return fluxes

    width = 2
    parts = blocks // width

    def solve_columns(part):
        chosen = spans[part * width : (part + 1) * width]
        values = []
        for here in chosen:
            surface, k = column_buffer[0, here, :], column_buffer[1, here, :]
            n1, w = params[1, here, :], params[2, here, :]
            value = (n1 + k * surface) * reciprocal(w + k)
            column_buffer[1, here, :] = value
            values.append(value)

        def substitute(level, values):
            values = [
                offset[level, here, :] + factor[level, here, :] * value
                for here, value in zip(chosen, values)
            ]
            for here, value in zip(chosen, values):
                column_buffer[level + 2, here, :] = value
            return values

        lax.fori_loop(0, upper, substitute, values, unroll=upper // 4)
        for t in range(part * width * SUB, (part + 1) * width * SUB):
            pltpu.make_async_copy(
                column_buffer.at[:, t, :],
                column_temp.at[:, pl.ds(t * LANES, LANES)],
                sems.at[part],
            ).start()

    lax.fori_loop(0, ITERS, over_columns, [zero] * blocks, unroll=2)
    early = min(2, parts)
    for part in range(early):
        solve_columns(part)
    lax.fori_loop(0, ITERS, over_land, [zero] * blocks, unroll=2)
    for i, here in enumerate(spans):
        surface = jnp.where(land_params(i)[3] > 0.0, warm[here, :], zero)
        for t in range(tiles):
            tile_buffer[t, here, :] = tile_base[t, here, :] + tile_slope[t, here, :] * surface
    for t in range(rows):
        pltpu.make_async_copy(
            tile_buffer.at[:, t, :], tile_temp.at[:, pl.ds(t * LANES, LANES)], tile_sem
        ).start()
    for part in range(early, parts):
        solve_columns(part)
    pltpu.make_async_copy(tile_buffer, tile_buffer, tile_sem).wait()
    for part in range(parts):
        span = column_buffer.at[:, pl.ds(part * width * SUB, width * SUB), :]
        pltpu.make_async_copy(span, span, sems.at[part]).wait()


def on_device(
    column_old,
    coupling,
    sea_temp,
    land_mask,
    tile_weight,
    tile_coeff,
    tile_capacity,
    tile_conduct,
    tile_old,
    tile_forcing,
):
    axes = ("lon", "lev")
    couplings, columns = coupling.shape
    levels = column_old.shape[0]
    tiles = tile_weight.shape[0]
    peers = lax.axis_size("lon")
    slot_count = columns // peers
    rows = columns // LANES
    blocks = rows // SUB
    fast = peers == SUB and rows == SUB * SUB
    devices = peers * lax.axis_size("lev")
    pairs = [(i, i ^ 1) for i in range(devices)]
    following = [(i, (i + 1 if i % 2 else i - 1) % devices) for i in range(devices)]
    hbm, vmem = pl.ANY, pltpu.VMEM
    full = (rows, LANES)
    mask = land_mask.reshape(full)
    table_outs = [
        VMEM(full, I32),
        VMEM(full, F32),
        VMEM(full, F32),
        VMEM((rows, 6 * rows), jnp.bfloat16),
        VMEM((2 * rows, 3 * rows), jnp.bfloat16),
        VMEM(full, I32),
    ]
    edge = (couplings, LANES)
    next_own, pair_own = chip_call(
        cut_edges,
        [VMEM(edge, F32)] * 2,
        [pltpu.HBM],
        [vmem] * 2,
        [DMA((2,))],
        (coupling,),
        pl.CostEstimate(flops=0, bytes_accessed=16 * couplings * LANES, transcendentals=0),
        EDGE_GRANT,
    )
    next_edge = lax.ppermute(next_own, axes, following)
    pair_edge = lax.ppermute(pair_own, axes, pairs)
    padded, source, first, second, place, fetch, spot = chip_call(
        functools.partial(prepare, fast),
        [VMEM((couplings, rows + 2 * SUB, LANES), F32)] + table_outs,
        [pltpu.HBM] * 2,
        [vmem] * 7,
        [VMEM(full, I32), DMA, DMA],
        (coupling, mask),
        pl.CostEstimate(
            flops=8 * couplings * columns, bytes_accessed=8 * levels * columns, transcendentals=0
        ),
        WIDE_GRANT,
    )
    sent = (peers, 6, SUB, LANES) if fast else (4,) + full
    handed = VMEM if fast else jax.ShapeDtypeStruct
    offset, factor, params, land, tile_base, tile_slope, send = chip_call(
        functools.partial(eliminate, fast),
        [
            VMEM((levels - 2,) + full, F32),
            VMEM((levels - 2,) + full, F32),
            VMEM((4,) + full, F32),
            handed((2,) + full, F32),
            VMEM((tiles,) + full, F32),
            VMEM((tiles,) + full, F32),
            handed(sent, F32),
        ],
        [vmem] * 8 + [pltpu.HBM] * 6,
        [vmem] * 7,
        [VMEM((couplings, LANES), F32)] * 2 + [VMEM((tiles, columns), F32)] * 6 + [DMA((6,))],
        (
            padded,
            on_chip(column_old),
            pair_edge,
            next_edge,
            source,
            first,
            second,
            place,
            tile_weight,
            tile_coeff,
            tile_capacity,
            tile_conduct,
            tile_old,
            tile_forcing,
        ),
        pl.CostEstimate(
            flops=20 * levels * columns, bytes_accessed=24 * tiles * columns, transcendentals=0
        ),
        TILE_GRANT,
    )
    if fast:
        inbox = lax.all_to_all(send, "lon", split_axis=0, concat_axis=0, tiled=True)
        slots = inbox
    else:
        ranked = send.reshape(4, slot_count, peers).transpose(2, 0, 1)
        own = land.reshape(2, peers, slot_count).transpose(1, 0, 2)
        got = lax.all_to_all(
            jnp.concatenate([own, ranked], axis=1), "lon", split_axis=0, concat_axis=0, tiled=True
        )
        inbox = got[:, :2].transpose(1, 2, 0).reshape((2,) + full)
        slots = got[:, 2:].transpose(1, 0, 2).reshape((4,) + full)
    width = 2
    column_temp, tile_temp = chip_call(
        functools.partial(finish, fast),
        [
            jax.ShapeDtypeStruct(column_old.shape, F32),
            jax.ShapeDtypeStruct(tile_old.shape, F32),
        ],
        [vmem] * 12,
        [hbm, hbm],
        [
            VMEM((2,) + full, F32),
            VMEM(full, F32),
            VMEM((levels,) + full, F32),
            VMEM((tiles,) + full, F32),
            DMA((blocks // width,)),
            DMA,
        ],
        (
            inbox,
            slots,
            offset,
            factor,
            params,
            land,
            tile_base,
            tile_slope,
            fetch,
            spot,
            mask,
            sea_temp.reshape(full),
        ),
        pl.CostEstimate(
            flops=4 * levels * columns, bytes_accessed=4 * levels * columns, transcendentals=0
        ),
    )
    return column_temp, tile_temp


def solution(mesh):
    wide, flat = P(None, ("lon", "lev")), P(("lon", "lev"))
    in_specs = (wide, wide, flat, flat) + (wide,) * 6
    return jax.shard_map(
        on_device, mesh=mesh, in_specs=in_specs, out_specs=(wide, wide), check_vma=False
    )
```

```python
import functools

import jax
import jax.numpy as jnp
from jax import lax
from jax.experimental import pallas as pl
from jax.experimental.pallas import tpu as pltpu
from jax.sharding import PartitionSpec as P


ITERS = 8
LANES = 128
SUB = 8
GRANT = 16 * 1024 * 1024
WIDE_GRANT = 55 * 1024 * 1024
EDGE_GRANT = 62 * 1024 * 1024
TILE_GRANT = 48 * 1024 * 1024
F32 = jnp.float32
I32 = jnp.int32
VMEM = pltpu.VMEM
DMA = pltpu.SemaphoreType.DMA


def on_chip(array):
    return pltpu.with_memory_space_constraint(array, pltpu.VMEM)


def chip_call(kernel, outs, in_spaces, out_spaces, scratch, args, cost, grant=GRANT):
    results = pl.pallas_call(
        kernel,
        out_shape=outs,
        in_specs=[pl.BlockSpec(memory_space=space) for space in in_spaces],
        out_specs=[pl.BlockSpec(memory_space=space) for space in out_spaces],
        scratch_shapes=scratch,
        cost_estimate=cost,
        compiler_params=pltpu.CompilerParams(vmem_limit_bytes=grant),
    )(*args)
    return [
        result if isinstance(out, jax.ShapeDtypeStruct) else on_chip(result)
        for result, out in zip(results, outs)
    ]


def lane_index(shape):
    return lax.broadcasted_iota(I32, shape, len(shape) - 1)


def row_index(shape):
    return lax.broadcasted_iota(I32, shape, len(shape) - 2)


def reciprocal(x):
    return 1.0 / x


def one_hot(condition):
    return jnp.where(condition, jnp.ones((), F32), jnp.zeros((), F32))


def spread(values):
    high = values.astype(jnp.bfloat16)
    rest = values - high.astype(F32)
    middle = rest.astype(jnp.bfloat16)
    low = (rest - middle.astype(F32)).astype(jnp.bfloat16)
    return jnp.concatenate([high, middle, low], axis=0)


def select_rows(chooser, values):
    return jnp.dot(chooser, spread(values), preferred_element_type=F32)


def count_dot(a, b):
    return jnp.dot(
        a.astype(jnp.bfloat16), b.astype(jnp.bfloat16), preferred_element_type=F32
    )


def lane_of(position, fast):
    return (position & 7) * 16 + (position >> 3) if fast else position


def position_of(lane, fast):
    return (lane & 15) * 8 + (lane >> 4) if fast else lane


def rank_row_of(row, fast):
    return (row & 7) * 8 + (row >> 3) if fast else row


def exchange(blocks):
    group = lane_index((SUB, LANES)) >> 4
    step = 1
    while step < SUB:
        high = (group & step) != 0
        done = list(blocks)
        for low in range(SUB):
            if low & step:
                continue
            a, b = blocks[low], blocks[low + step]
            done[low] = jnp.where(high, pltpu.roll(b, 16 * step, 1), a)
            done[low + step] = jnp.where(high, b, pltpu.roll(a, LANES - 16 * step, 1))
        blocks = done
        step *= 2
    return blocks


def build_tables(fast, mask, source_ref, first_ref, second_ref, place_ref, fetch_ref, spot_ref):
    rows = mask.shape[0]
    shape = (rows, LANES)
    land = mask.astype(F32)
    upper = one_hot(row_index((LANES, LANES)) <= lane_index((LANES, LANES)))
    running = count_dot(land, upper)
    totals = count_dot(land, jnp.ones((LANES, LANES), F32))
    before = one_hot(lane_index((rows, rows)) < row_index((rows, rows)))
    base = count_dot(before, totals).astype(I32)
    totals = totals.astype(I32)
    running = running.astype(I32)
    start = base & (LANES - 1)
    position = position_of(lane_index(shape), fast)
    ordinal = (position - start) & (LANES - 1)
    source = jnp.zeros(shape, I32)
    step = LANES // 2
    while step:
        reached = jnp.take_along_axis(running, source + (step - 1), axis=1)
        source = jnp.where(reached <= ordinal, source + step, source)
        step //= 2
    source_ref[...] = source
    valid = ordinal < totals
    first_ref[...] = one_hot(valid & (position >= start))
    second_ref[...] = one_hot(valid & (position < start))
    row_totals = lax.dot_general(
        jnp.ones((SUB, LANES), jnp.bfloat16),
        land.astype(jnp.bfloat16),
        (((1,), (1,)), ((), ())),
        preferred_element_type=F32,
    )
    earlier = one_hot(row_index((rows, rows)) < lane_index((rows, rows)))
    base_row = count_dot(row_totals, earlier).astype(I32)[:1]
    lead_row = jnp.broadcast_to(base_row >> 7, (rows, rows))
    wanted = rank_row_of(row_index((rows, rows)), fast)
    place_ref[...] = jnp.concatenate(
        [one_hot(lead_row == wanted), one_hot(lead_row + 1 == wanted)] * 3, axis=1
    ).astype(jnp.bfloat16)
    lead = (base >> 7)[:, :rows] if rows <= LANES else base[:, :1] >> 7
    held = rank_row_of(lane_index((rows, rows)), fast)
    chooser = jnp.concatenate([one_hot(lead == held), one_hot(lead + 1 == held)], axis=0)
    fetch_ref[...] = jnp.concatenate([chooser] * 3, axis=1).astype(jnp.bfloat16)
    spot = start + running - 1
    spot_ref[...] = lane_of(spot & (LANES - 1), fast) + (spot & LANES)


def is_even():
    return lax.rem(lax.axis_index("lon") * lax.axis_size("lev") + lax.axis_index("lev"), 2) == 0


def cut_edges(coupling, next_edge, pair_edge, sems):
    last = coupling.shape[1] - LANES
    even = is_even()
    near = pl.multiple_of(jnp.where(even, last, 0), LANES)
    far = pl.multiple_of(jnp.where(even, 0, last), LANES)
    copies = [
        pltpu.make_async_copy(coupling.at[:, pl.ds(far, LANES)], next_edge, sems.at[0]),
        pltpu.make_async_copy(coupling.at[:, pl.ds(near, LANES)], pair_edge, sems.at[1]),
    ]
    for copy in copies:
        copy.start()
    for copy in copies:
        copy.wait()


def prepare(
    fast, coupling, mask, padded, source, first, second, place, fetch, spot, held, sem, mask_sem
):
    levels, height, _ = padded.shape
    rows = height - 2 * SUB
    mask_copy = pltpu.make_async_copy(mask, held, mask_sem)
    mask_copy.start()
    for t in range(rows):
        pltpu.make_async_copy(
            coupling.at[:, pl.ds(t * LANES, LANES)], padded.at[:, SUB + t, :], sem
        ).start()
    blank = jnp.zeros((SUB, LANES), F32)

    def clear(level, carried):
        padded[level, pl.ds(0, SUB), :] = blank
        padded[level, pl.ds(SUB + rows, SUB), :] = blank
        return carried

    lax.fori_loop(0, levels, clear, 0, unroll=3)
    mask_copy.wait()
    build_tables(fast, held[...], source, first, second, place, fetch, spot)
    inner = padded.at[:, pl.ds(SUB, rows), :]
    pltpu.make_async_copy(inner, inner, sem).wait()


def eliminate(
    fast,
    padded,
    old,
    pair_edge,
    next_edge,
    source,
    first,
    second,
    place,
    tile_weight,
    tile_coeff,
    tile_capacity,
    tile_conduct,
    tile_old,
    tile_forcing,
    offset,
    factor,
    params,
    land,
    tile_base,
    tile_slope,
    send,
    low_edge,
    high_edge,
    weight,
    coeff,
    capacity,
    conduct,
    before,
    forcing,
    sems,
):
    levels, height, _ = padded.shape
    rows = height - 2 * SUB
    blocks = rows // SUB
    copies = [
        pltpu.make_async_copy(source_tile, buffer, sems.at[n])
        for n, (source_tile, buffer) in enumerate(
            (
                (tile_weight, weight),
                (tile_coeff, coeff),
                (tile_capacity, capacity),
                (tile_conduct, conduct),
                (tile_old, before),
                (tile_forcing, forcing),
            )
        )
    ]
    for copy in copies:
        copy.start()
    even = is_even()

    def turn(rows_here):
        pair, following = pair_edge[rows_here, :], next_edge[rows_here, :]
        low = jnp.where(even, following, pair)
        high = jnp.where(even, pair, following)
        low_edge[rows_here, :] = pltpu.roll(low, 1, 1) * 0.25
        high_edge[rows_here, :] = pltpu.roll(high, LANES - 1, 1) * 0.25

    half = levels // (2 * SUB) * SUB

    def turn_half(index, carried):
        turn(pl.ds(pl.multiple_of(index * half, SUB), half))
        return carried

    lax.fori_loop(0, 2, turn_half, 0)
    if levels > 2 * half:
        turn(pl.ds(2 * half, levels - 2 * half))
    row, lane = row_index((SUB, LANES)), lane_index((SUB, LANES))
    low_corner = (row == 0) & (lane == 0)
    high_corner = (row == SUB - 1) & (lane == LANES - 1)
    at_last, at_first = lane == LANES - 1, lane == 0
    blank = jnp.zeros((SUB, LANES), F32)

    def smooth_at(level):
        values = []
        for g in range(blocks):
            top = SUB + g * SUB
            here = padded[level, pl.ds(top, SUB), :]
            above = padded[level, pl.ds(top - 1, SUB), :]
            below = padded[level, pl.ds(top + 1, SUB), :]
            left = pltpu.roll(jnp.where(at_last, above, here), 1, 1)
            right = pltpu.roll(jnp.where(at_first, below, here), LANES - 1, 1)
            values.append((left + right) * 0.25 + here * 0.5)
        low = jnp.broadcast_to(low_edge[pl.ds(level, 1), :], (SUB, LANES))
        high = jnp.broadcast_to(high_edge[pl.ds(level, 1), :], (SUB, LANES))
        values[0] = values[0] + jnp.where(low_corner, low, blank)
        values[-1] = values[-1] + jnp.where(high_corner, high, blank)
        return values

    def old_at(level, g):
        return old[level, pl.ds(g * SUB * LANES, SUB * LANES)].reshape(SUB, LANES)

    def step(level, carried):
        conduct_u, right_n = carried
        below = smooth_at(level - 1)
        next_u, next_n = [], []
        for g in range(blocks):
            inverse = reciprocal(conduct_u[g] + below[g])
            e = right_n[g] * inverse
            offset[level - 2, pl.ds(g * SUB, SUB), :] = e
            f = below[g] * inverse
            factor[level - 2, pl.ds(g * SUB, SUB), :] = f
            next_u.append(1.0 + f * conduct_u[g])
            next_n.append(old_at(level - 1, g) + f * right_n[g])
        return next_u, next_n

    top = [old_at(levels, g) for g in range(blocks)]
    ones = [jnp.ones((SUB, LANES), F32) for _ in range(blocks)]
    conduct_u, right_n = ones, top
    for level in range(levels, 1, -1):
        conduct_u, right_n = step(level, (conduct_u, right_n))
    ground = smooth_at(0)
    for g in range(blocks):
        here = pl.ds(g * SUB, SUB)
        params[0, here, :] = old_at(0, g)
        params[1, here, :] = right_n[g]
        params[2, here, :] = conduct_u[g]
        params[3, here, :] = ground[g]
    pick, lead, rest = source[...], first[...], second[...]
    halves = []
    for n in range(4):
        moved = jnp.take_along_axis(params[n], pick, axis=1)
        halves.append(jnp.concatenate([moved * lead, moved * rest], axis=0))
    packed = select_rows(place[...], jnp.concatenate(halves, axis=1))
    for n in range(4):
        field = packed[:, n * LANES : (n + 1) * LANES]
        if fast:
            for k, block in enumerate(exchange([field[g * SUB : (g + 1) * SUB] for g in range(blocks)])):
                send[k, 2 + n] = block
        else:
            send[n] = field
    for copy in copies:
        copy.wait()
    tiles = weight.shape[0]

    def tile_block(g, carried):
        columns = pl.ds(pl.multiple_of(g * SUB * LANES, SUB * LANES), SUB * LANES)
        here = pl.ds(pl.multiple_of(g * SUB, SUB), SUB)
        weight_sum = land_a = land_b = blank
        for t in range(tiles):
            w, c, cap, con, was, force = (
                buffer[t, columns].reshape(SUB, LANES)
                for buffer in (weight, coeff, capacity, conduct, before, forcing)
            )
            keep = cap + con
            inverse = reciprocal(keep + c)
            src = cap * was + force
            slope = c * inverse
            tile_base[t, here, :] = src * inverse
            tile_slope[t, here, :] = slope
            share = w * slope
            weight_sum = weight_sum + w
            land_a = land_a + share * src
            land_b = land_b + share * keep
        inverse = reciprocal(weight_sum)
        land[0, here, :] = land_a * inverse
        land[1, here, :] = land_b * inverse
        return carried

    lax.fori_loop(0, blocks, tile_block, 0, unroll=True)
    if fast:
        for k in range(blocks):
            for n in range(2):
                send[k, n] = land[n, pl.ds(k * SUB, SUB), :]


def finish(
    fast,
    inbox,
    slots,
    offset,
    factor,
    params,
    land,
    tile_base,
    tile_slope,
    fetch,
    spot,
    mask,
    sea,
    column_temp,
    tile_temp,
    solved,
    warm,
    ground_pair,
    column_buffer,
    tile_buffer,
    sems,
    tile_sem,
):
    upper, rows, _ = offset.shape
    blocks = rows // SUB
    tiles = tile_base.shape[0]
    fields = []
    for n in range(2):
        if fast:
            fields.append(
                jnp.concatenate(exchange([inbox[k, n] for k in range(blocks)]), axis=0)
            )
        else:
            fields.append(inbox[n])
    windows = select_rows(fetch[...], jnp.concatenate(fields, axis=1))
    place = spot[...]
    lane, upper_half = place & (LANES - 1), place >= LANES
    is_land = mask[...] == 1
    for n, ocean in ((0, sea[...]), (1, jnp.ones((rows, LANES), F32))):
        one = windows[:rows, n * LANES : (n + 1) * LANES]
        two = windows[rows:, n * LANES : (n + 1) * LANES]
        found = jnp.where(
            upper_half,
            jnp.take_along_axis(two, lane, axis=1),
            jnp.take_along_axis(one, lane, axis=1),
        )
        solved[n] = jnp.where(is_land, found, ocean)

    def update(a, b, base, n1, w, ground, flux):
        k = ground * (1.0 + 0.5 * jnp.tanh(flux))
        total = w + k
        surface = ((base + a) * total + k * n1) * reciprocal((1.0 + b) * total + w * k)
        return k, surface, a - b * surface

    zero = jnp.zeros((SUB, LANES), F32)
    spans = [pl.ds(g * SUB, SUB) for g in range(blocks)]

    def over_columns(repeat, flux):
        fluxes = []
        for here, last in zip(spans, flux):
            k, surface, next_flux = update(
                solved[0, here, :], solved[1, here, :], *(params[n, here, :] for n in range(4)), last
            )
            ground_pair[0, here, :] = surface
            ground_pair[1, here, :] = k
            fluxes.append(next_flux)
        return fluxes

    def land_params(i):
        return [inbox[i, 2 + n] if fast else slots[n, spans[i], :] for n in range(4)]

    def over_land(repeat, flux):
        fluxes = []
        for i, (here, last) in enumerate(zip(spans, flux)):
            base, n1, w, ground = land_params(i)
            w = jnp.where(ground > 0.0, w, 1.0)
            _, surface, next_flux = update(
                land[0, here, :], land[1, here, :], base, n1, w, ground, last
            )
            warm[here, :] = surface
            fluxes.append(next_flux)
        return fluxes

    width = 2
    parts = blocks // width

    def put(level, g, value):
        column_buffer[level, pl.ds(g * SUB * LANES, SUB * LANES)] = value.reshape(SUB * LANES)

    def solve_columns(part):
        chosen = range(part * width, (part + 1) * width)
        values = []
        for g in chosen:
            here = spans[g]
            surface, k = ground_pair[0, here, :], ground_pair[1, here, :]
            n1, w = params[1, here, :], params[2, here, :]
            value = (n1 + k * surface) * reciprocal(w + k)
            put(0, g, surface)
            put(1, g, value)
            values.append(value)
        for level in range(upper):
            for n, g in enumerate(chosen):
                here = spans[g]
                values[n] = offset[level, here, :] + factor[level, here, :] * values[n]
                put(level + 2, g, values[n])
        part_copy(part).start()

    def part_copy(part):
        area = pl.ds(part * width * SUB * LANES, width * SUB * LANES)
        return pltpu.make_async_copy(
            column_buffer.at[:, area], column_temp.at[:, area], sems.at[part]
        )

    lax.fori_loop(0, ITERS, over_columns, [zero] * blocks, unroll=2)
    early = min(2, parts)
    for part in range(early):
        solve_columns(part)
    lax.fori_loop(0, ITERS, over_land, [zero] * blocks, unroll=2)
    for i, here in enumerate(spans):
        surface = jnp.where(land_params(i)[3] > 0.0, warm[here, :], zero)
        for t in range(tiles):
            tile_buffer[t, here, :] = tile_base[t, here, :] + tile_slope[t, here, :] * surface
    for t in range(rows):
        pltpu.make_async_copy(
            tile_buffer.at[:, t, :], tile_temp.at[:, pl.ds(t * LANES, LANES)], tile_sem
        ).start()
    for part in range(early, parts):
        solve_columns(part)
    pltpu.make_async_copy(tile_buffer, tile_buffer, tile_sem).wait()
    for part in range(parts):
        part_copy(part).wait()


def on_device(
    column_old,
    coupling,
    sea_temp,
    land_mask,
    tile_weight,
    tile_coeff,
    tile_capacity,
    tile_conduct,
    tile_old,
    tile_forcing,
):
    axes = ("lon", "lev")
    couplings, columns = coupling.shape
    levels = column_old.shape[0]
    tiles = tile_weight.shape[0]
    peers = lax.axis_size("lon")
    slot_count = columns // peers
    rows = columns // LANES
    blocks = rows // SUB
    fast = peers == SUB and rows == SUB * SUB
    devices = peers * lax.axis_size("lev")
    pairs = [(i, i ^ 1) for i in range(devices)]
    following = [(i, (i + 1 if i % 2 else i - 1) % devices) for i in range(devices)]
    hbm, vmem = pl.ANY, pltpu.VMEM
    full = (rows, LANES)
    mask = land_mask.reshape(full)
    table_outs = [
        VMEM(full, I32),
        VMEM(full, F32),
        VMEM(full, F32),
        VMEM((rows, 6 * rows), jnp.bfloat16),
        VMEM((2 * rows, 3 * rows), jnp.bfloat16),
        VMEM(full, I32),
    ]
    edge = (couplings, LANES)
    next_own, pair_own = chip_call(
        cut_edges,
        [VMEM(edge, F32)] * 2,
        [pltpu.HBM],
        [vmem] * 2,
        [DMA((2,))],
        (coupling,),
        pl.CostEstimate(flops=0, bytes_accessed=16 * couplings * LANES, transcendentals=0),
        EDGE_GRANT,
    )
    next_edge = lax.ppermute(next_own, axes, following)
    pair_edge = lax.ppermute(pair_own, axes, pairs)
    padded, source, first, second, place, fetch, spot = chip_call(
        functools.partial(prepare, fast),
        [VMEM((couplings, rows + 2 * SUB, LANES), F32)] + table_outs,
        [pltpu.HBM] * 2,
        [vmem] * 7,
        [VMEM(full, I32), DMA, DMA],
        (coupling, mask),
        pl.CostEstimate(
            flops=8 * couplings * columns, bytes_accessed=8 * levels * columns, transcendentals=0
        ),
        WIDE_GRANT,
    )
    sent = (peers, 6, SUB, LANES) if fast else (4,) + full
    handed = VMEM if fast else jax.ShapeDtypeStruct
    offset, factor, params, land, tile_base, tile_slope, send = chip_call(
        functools.partial(eliminate, fast),
        [
            VMEM((levels - 2,) + full, F32),
            VMEM((levels - 2,) + full, F32),
            VMEM((4,) + full, F32),
            handed((2,) + full, F32),
            VMEM((tiles,) + full, F32),
            VMEM((tiles,) + full, F32),
            handed(sent, F32),
        ],
        [vmem] * 8 + [pltpu.HBM] * 6,
        [vmem] * 7,
        [VMEM((couplings, LANES), F32)] * 2 + [VMEM((tiles, columns), F32)] * 6 + [DMA((6,))],
        (
            padded,
            on_chip(column_old),
            pair_edge,
            next_edge,
            source,
            first,
            second,
            place,
            tile_weight,
            tile_coeff,
            tile_capacity,
            tile_conduct,
            tile_old,
            tile_forcing,
        ),
        pl.CostEstimate(
            flops=20 * levels * columns, bytes_accessed=24 * tiles * columns, transcendentals=0
        ),
        TILE_GRANT,
    )
    if fast:
        inbox = lax.all_to_all(send, "lon", split_axis=0, concat_axis=0, tiled=True)
        slots = inbox
    else:
        ranked = send.reshape(4, slot_count, peers).transpose(2, 0, 1)
        own = land.reshape(2, peers, slot_count).transpose(1, 0, 2)
        got = lax.all_to_all(
            jnp.concatenate([own, ranked], axis=1), "lon", split_axis=0, concat_axis=0, tiled=True
        )
        inbox = got[:, :2].transpose(1, 2, 0).reshape((2,) + full)
        slots = got[:, 2:].transpose(1, 0, 2).reshape((4,) + full)
    width = 2
    column_temp, tile_temp = chip_call(
        functools.partial(finish, fast),
        [
            jax.ShapeDtypeStruct(column_old.shape, F32),
            jax.ShapeDtypeStruct(tile_old.shape, F32),
        ],
        [vmem] * 12,
        [hbm, hbm],
        [
            VMEM((2,) + full, F32),
            VMEM(full, F32),
            VMEM((2,) + full, F32),
            VMEM((levels, columns), F32),
            VMEM((tiles,) + full, F32),
            DMA((blocks // width,)),
            DMA,
        ],
        (
            inbox,
            slots,
            offset,
            factor,
            params,
            land,
            tile_base,
            tile_slope,
            fetch,
            spot,
            mask,
            sea_temp.reshape(full),
        ),
        pl.CostEstimate(
            flops=4 * levels * columns, bytes_accessed=4 * levels * columns, transcendentals=0
        ),
    )
    return column_temp, tile_temp


def solution(mesh):
    wide, flat = P(None, ("lon", "lev")), P(("lon", "lev"))
    in_specs = (wide, wide, flat, flat) + (wide,) * 6
    return jax.shard_map(
        on_device, mesh=mesh, in_specs=in_specs, out_specs=(wide, wide), check_vma=False
    )
```

```python
import functools

import jax
import jax.numpy as jnp
from jax import lax
from jax.experimental import pallas as pl
from jax.experimental.pallas import tpu as pltpu
from jax.sharding import PartitionSpec as P


ITERS = 8
LANES = 128
SUB = 8
GRANT = 16 * 1024 * 1024
WIDE_GRANT = 55 * 1024 * 1024
EDGE_GRANT = 62 * 1024 * 1024
TILE_GRANT = 48 * 1024 * 1024
F32 = jnp.float32
I32 = jnp.int32
VMEM = pltpu.VMEM
DMA = pltpu.SemaphoreType.DMA


def on_chip(array):
    return pltpu.with_memory_space_constraint(array, pltpu.VMEM)


def chip_call(kernel, outs, in_spaces, out_spaces, scratch, args, cost, grant=GRANT):
    results = pl.pallas_call(
        kernel,
        out_shape=outs,
        in_specs=[pl.BlockSpec(memory_space=space) for space in in_spaces],
        out_specs=[pl.BlockSpec(memory_space=space) for space in out_spaces],
        scratch_shapes=scratch,
        cost_estimate=cost,
        compiler_params=pltpu.CompilerParams(vmem_limit_bytes=grant),
    )(*args)
    return [
        result if isinstance(out, jax.ShapeDtypeStruct) else on_chip(result)
        for result, out in zip(results, outs)
    ]


def lane_index(shape):
    return lax.broadcasted_iota(I32, shape, len(shape) - 1)


def row_index(shape):
    return lax.broadcasted_iota(I32, shape, len(shape) - 2)


def reciprocal(x):
    return 1.0 / x


def one_hot(condition):
    return jnp.where(condition, jnp.ones((), F32), jnp.zeros((), F32))


def spread(values):
    high = values.astype(jnp.bfloat16)
    rest = values - high.astype(F32)
    middle = rest.astype(jnp.bfloat16)
    low = (rest - middle.astype(F32)).astype(jnp.bfloat16)
    return jnp.concatenate([high, middle, low], axis=0)


def select_rows(chooser, values):
    return jnp.dot(chooser, spread(values), preferred_element_type=F32)


def count_dot(a, b):
    return jnp.dot(
        a.astype(jnp.bfloat16), b.astype(jnp.bfloat16), preferred_element_type=F32
    )


def lane_of(position, fast):
    return (position & 7) * 16 + (position >> 3) if fast else position


def position_of(lane, fast):
    return (lane & 15) * 8 + (lane >> 4) if fast else lane


def rank_row_of(row, fast):
    return (row & 7) * 8 + (row >> 3) if fast else row


def exchange(blocks):
    group = lane_index((SUB, LANES)) >> 4
    step = 1
    while step < SUB:
        high = (group & step) != 0
        done = list(blocks)
        for low in range(SUB):
            if low & step:
                continue
            a, b = blocks[low], blocks[low + step]
            done[low] = jnp.where(high, pltpu.roll(b, 16 * step, 1), a)
            done[low + step] = jnp.where(high, b, pltpu.roll(a, LANES - 16 * step, 1))
        blocks = done
        step *= 2
    return blocks


def build_tables(fast, mask, source_ref, first_ref, second_ref, place_ref, fetch_ref, spot_ref):
    rows = mask.shape[0]
    shape = (rows, LANES)
    land = mask.astype(F32)
    upper = one_hot(row_index((LANES, LANES)) <= lane_index((LANES, LANES)))
    running = count_dot(land, upper)
    totals = count_dot(land, jnp.ones((LANES, LANES), F32))
    before = one_hot(lane_index((rows, rows)) < row_index((rows, rows)))
    base = count_dot(before, totals).astype(I32)
    totals = totals.astype(I32)
    running = running.astype(I32)
    start = base & (LANES - 1)
    position = position_of(lane_index(shape), fast)
    ordinal = (position - start) & (LANES - 1)
    source = jnp.zeros(shape, I32)
    step = LANES // 2
    while step:
        reached = jnp.take_along_axis(running, source + (step - 1), axis=1)
        source = jnp.where(reached <= ordinal, source + step, source)
        step //= 2
    source_ref[...] = source
    valid = ordinal < totals
    first_ref[...] = one_hot(valid & (position >= start))
    second_ref[...] = one_hot(valid & (position < start))
    row_totals = lax.dot_general(
        jnp.ones((SUB, LANES), jnp.bfloat16),
        land.astype(jnp.bfloat16),
        (((1,), (1,)), ((), ())),
        preferred_element_type=F32,
    )
    earlier = one_hot(row_index((rows, rows)) < lane_index((rows, rows)))
    base_row = count_dot(row_totals, earlier).astype(I32)[:1]
    lead_row = jnp.broadcast_to(base_row >> 7, (rows, rows))
    wanted = rank_row_of(row_index((rows, rows)), fast)
    place_ref[...] = jnp.concatenate(
        [one_hot(lead_row == wanted), one_hot(lead_row + 1 == wanted)] * 3, axis=1
    ).astype(jnp.bfloat16)
    lead = (base >> 7)[:, :rows] if rows <= LANES else base[:, :1] >> 7
    held = rank_row_of(lane_index((rows, rows)), fast)
    chooser = jnp.concatenate([one_hot(lead == held), one_hot(lead + 1 == held)], axis=0)
    fetch_ref[...] = jnp.concatenate([chooser] * 3, axis=1).astype(jnp.bfloat16)
    spot = start + running - 1
    spot_ref[...] = lane_of(spot & (LANES - 1), fast) + (spot & LANES)


def is_even():
    return lax.rem(lax.axis_index("lon") * lax.axis_size("lev") + lax.axis_index("lev"), 2) == 0


def cut_edges(coupling, next_edge, pair_edge, sems):
    last = coupling.shape[1] - LANES
    even = is_even()
    near = pl.multiple_of(jnp.where(even, last, 0), LANES)
    far = pl.multiple_of(jnp.where(even, 0, last), LANES)
    copies = [
        pltpu.make_async_copy(coupling.at[:, pl.ds(far, LANES)], next_edge, sems.at[0]),
        pltpu.make_async_copy(coupling.at[:, pl.ds(near, LANES)], pair_edge, sems.at[1]),
    ]
    for copy in copies:
        copy.start()
    for copy in copies:
        copy.wait()


def prepare(
    fast, coupling, mask, padded, source, first, second, place, fetch, spot, held, sem, mask_sem
):
    levels, height, _ = padded.shape
    rows = height - 2 * SUB
    mask_copy = pltpu.make_async_copy(mask, held, mask_sem)
    mask_copy.start()
    for t in range(rows):
        pltpu.make_async_copy(
            coupling.at[:, pl.ds(t * LANES, LANES)], padded.at[:, SUB + t, :], sem
        ).start()
    blank = jnp.zeros((SUB, LANES), F32)

    def clear(level, carried):
        padded[level, pl.ds(0, SUB), :] = blank
        padded[level, pl.ds(SUB + rows, SUB), :] = blank
        return carried

    lax.fori_loop(0, levels, clear, 0, unroll=3)
    mask_copy.wait()
    build_tables(fast, held[...], source, first, second, place, fetch, spot)
    inner = padded.at[:, pl.ds(SUB, rows), :]
    pltpu.make_async_copy(inner, inner, sem).wait()


def eliminate(
    fast,
    padded,
    old,
    pair_edge,
    next_edge,
    source,
    first,
    second,
    place,
    tile_weight,
    tile_coeff,
    tile_capacity,
    tile_conduct,
    tile_old,
    tile_forcing,
    offset,
    factor,
    params,
    land,
    tile_base,
    tile_slope,
    send,
    low_edge,
    high_edge,
    weight,
    coeff,
    capacity,
    conduct,
    before,
    forcing,
    sems,
):
    levels, height, _ = padded.shape
    rows = height - 2 * SUB
    blocks = rows // SUB
    copies = [
        pltpu.make_async_copy(source_tile, buffer, sems.at[n])
        for n, (source_tile, buffer) in enumerate(
            (
                (tile_weight, weight),
                (tile_coeff, coeff),
                (tile_capacity, capacity),
                (tile_conduct, conduct),
                (tile_old, before),
                (tile_forcing, forcing),
            )
        )
    ]
    for copy in copies:
        copy.start()
    even = is_even()

    def turn(rows_here):
        pair, following = pair_edge[rows_here, :], next_edge[rows_here, :]
        low = jnp.where(even, following, pair)
        high = jnp.where(even, pair, following)
        low_edge[rows_here, :] = pltpu.roll(low, 1, 1) * 0.25
        high_edge[rows_here, :] = pltpu.roll(high, LANES - 1, 1) * 0.25

    half = levels // (2 * SUB) * SUB

    def turn_half(index, carried):
        turn(pl.ds(pl.multiple_of(index * half, SUB), half))
        return carried

    lax.fori_loop(0, 2, turn_half, 0)
    if levels > 2 * half:
        turn(pl.ds(2 * half, levels - 2 * half))
    row, lane = row_index((SUB, LANES)), lane_index((SUB, LANES))
    low_corner = (row == 0) & (lane == 0)
    high_corner = (row == SUB - 1) & (lane == LANES - 1)
    at_last, at_first = lane == LANES - 1, lane == 0
    blank = jnp.zeros((SUB, LANES), F32)

    def smooth_at(level):
        values = []
        for g in range(blocks):
            top = SUB + g * SUB
            here = padded[level, pl.ds(top, SUB), :]
            above = padded[level, pl.ds(top - 1, SUB), :]
            below = padded[level, pl.ds(top + 1, SUB), :]
            left = pltpu.roll(jnp.where(at_last, above, here), 1, 1)
            right = pltpu.roll(jnp.where(at_first, below, here), LANES - 1, 1)
            values.append((left + right) * 0.25 + here * 0.5)
        low = jnp.broadcast_to(low_edge[pl.ds(level, 1), :], (SUB, LANES))
        high = jnp.broadcast_to(high_edge[pl.ds(level, 1), :], (SUB, LANES))
        values[0] = values[0] + jnp.where(low_corner, low, blank)
        values[-1] = values[-1] + jnp.where(high_corner, high, blank)
        return values

    def old_at(level, g):
        return old[level, pl.ds(g * SUB * LANES, SUB * LANES)].reshape(SUB, LANES)

    def step(level, carried):
        conduct_u, right_n = carried
        below = smooth_at(level - 1)
        next_u, next_n = [], []
        for g in range(blocks):
            inverse = reciprocal(conduct_u[g] + below[g])
            e = right_n[g] * inverse
            offset[level - 2, pl.ds(g * SUB, SUB), :] = e
            f = below[g] * inverse
            factor[level - 2, pl.ds(g * SUB, SUB), :] = f
            next_u.append(1.0 + f * conduct_u[g])
            next_n.append(old_at(level - 1, g) + f * right_n[g])
        return next_u, next_n

    top = [old_at(levels, g) for g in range(blocks)]
    ones = [jnp.ones((SUB, LANES), F32) for _ in range(blocks)]
    conduct_u, right_n = ones, top
    for level in range(levels, 1, -1):
        conduct_u, right_n = step(level, (conduct_u, right_n))
    ground = smooth_at(0)
    for g in range(blocks):
        here = pl.ds(g * SUB, SUB)
        params[0, here, :] = old_at(0, g)
        params[1, here, :] = right_n[g]
        params[2, here, :] = conduct_u[g]
        params[3, here, :] = ground[g]
    pick, lead, rest = source[...], first[...], second[...]
    halves = []
    for n in range(4):
        moved = jnp.take_along_axis(params[n], pick, axis=1)
        halves.append(jnp.concatenate([moved * lead, moved * rest], axis=0))
    packed = select_rows(place[...], jnp.concatenate(halves, axis=1))
    for n in range(4):
        field = packed[:, n * LANES : (n + 1) * LANES]
        if fast:
            for k, block in enumerate(exchange([field[g * SUB : (g + 1) * SUB] for g in range(blocks)])):
                send[k, 2 + n] = block
        else:
            send[n] = field
    for copy in copies:
        copy.wait()
    tiles = weight.shape[0]

    def tile_block(g, carried):
        columns = pl.ds(pl.multiple_of(g * SUB * LANES, SUB * LANES), SUB * LANES)
        here = pl.ds(pl.multiple_of(g * SUB, SUB), SUB)
        weight_sum = land_a = land_b = blank
        for t in range(tiles):
            w, c, cap, con, was, force = (
                buffer[t, columns].reshape(SUB, LANES)
                for buffer in (weight, coeff, capacity, conduct, before, forcing)
            )
            keep = cap + con
            inverse = reciprocal(keep + c)
            src = cap * was + force
            slope = c * inverse
            tile_base[t, here, :] = src * inverse
            tile_slope[t, here, :] = slope
            share = w * slope
            weight_sum = weight_sum + w
            land_a = land_a + share * src
            land_b = land_b + share * keep
        inverse = reciprocal(weight_sum)
        land[0, here, :] = land_a * inverse
        land[1, here, :] = land_b * inverse
        return carried

    lax.fori_loop(0, blocks, tile_block, 0, unroll=True)
    if fast:
        for k in range(blocks):
            for n in range(2):
                send[k, n] = land[n, pl.ds(k * SUB, SUB), :]


def finish(
    fast,
    inbox,
    slots,
    offset,
    factor,
    params,
    land,
    tile_base,
    tile_slope,
    fetch,
    spot,
    mask,
    sea,
    column_temp,
    tile_temp,
    solved,
    warm,
    ground_pair,
    column_buffer,
    tile_buffer,
    sems,
    tile_sem,
):
    upper, rows, _ = offset.shape
    blocks = rows // SUB
    tiles = tile_base.shape[0]
    fields = []
    for n in range(2):
        if fast:
            fields.append(
                jnp.concatenate(exchange([inbox[k, n] for k in range(blocks)]), axis=0)
            )
        else:
            fields.append(inbox[n])
    windows = select_rows(fetch[...], jnp.concatenate(fields, axis=1))
    place = spot[...]
    lane, upper_half = place & (LANES - 1), place >= LANES
    is_land = mask[...] == 1
    for n, ocean in ((0, sea[...]), (1, jnp.ones((rows, LANES), F32))):
        one = windows[:rows, n * LANES : (n + 1) * LANES]
        two = windows[rows:, n * LANES : (n + 1) * LANES]
        found = jnp.where(
            upper_half,
            jnp.take_along_axis(two, lane, axis=1),
            jnp.take_along_axis(one, lane, axis=1),
        )
        solved[n] = jnp.where(is_land, found, ocean)

    def update(a, b, base, n1, w, ground, flux):
        k = ground * (1.0 + 0.5 * jnp.tanh(flux))
        total = w + k
        surface = ((base + a) * total + k * n1) * reciprocal((1.0 + b) * total + w * k)
        return k, surface, a - b * surface

    zero = jnp.zeros((SUB, LANES), F32)
    spans = [pl.ds(g * SUB, SUB) for g in range(blocks)]

    def over_columns(repeat, flux):
        fluxes = []
        for here, last in zip(spans, flux):
            k, surface, next_flux = update(
                solved[0, here, :], solved[1, here, :], *(params[n, here, :] for n in range(4)), last
            )
            ground_pair[0, here, :] = surface
            ground_pair[1, here, :] = k
            fluxes.append(next_flux)
        return fluxes

    def land_params(i):
        return [inbox[i, 2 + n] if fast else slots[n, spans[i], :] for n in range(4)]

    def over_land(repeat, flux):
        fluxes = []
        for i, (here, last) in enumerate(zip(spans, flux)):
            base, n1, w, ground = land_params(i)
            w = jnp.where(ground > 0.0, w, 1.0)
            _, surface, next_flux = update(
                land[0, here, :], land[1, here, :], base, n1, w, ground, last
            )
            warm[here, :] = surface
            fluxes.append(next_flux)
        return fluxes

    width = 2
    parts = blocks // width

    def put(level, g, value):
        column_buffer[level, pl.ds(g * SUB * LANES, SUB * LANES)] = value.reshape(SUB * LANES)

    def solve_columns(part):
        chosen = range(part * width, (part + 1) * width)
        values = []
        for g in chosen:
            here = spans[g]
            surface, k = ground_pair[0, here, :], ground_pair[1, here, :]
            n1, w = params[1, here, :], params[2, here, :]
            value = (n1 + k * surface) * reciprocal(w + k)
            put(0, g, surface)
            put(1, g, value)
            values.append(value)
        for level in range(upper):
            for n, g in enumerate(chosen):
                here = spans[g]
                values[n] = offset[level, here, :] + factor[level, here, :] * values[n]
                put(level + 2, g, values[n])
        part_copy(part).start()

    def part_copy(part):
        area = pl.ds(part * width * SUB * LANES, width * SUB * LANES)
        return pltpu.make_async_copy(
            column_buffer.at[:, area], column_temp.at[:, area], sems.at[part]
        )

    lax.fori_loop(0, ITERS, over_columns, [zero] * blocks, unroll=2)
    early = min(2, parts)
    for part in range(early):
        solve_columns(part)
    lax.fori_loop(0, ITERS, over_land, [zero] * blocks, unroll=2)
    for i, here in enumerate(spans):
        surface = jnp.where(land_params(i)[3] > 0.0, warm[here, :], zero)
        for t in range(tiles):
            value = tile_base[t, here, :] + tile_slope[t, here, :] * surface
            tile_buffer[t, pl.ds(i * SUB * LANES, SUB * LANES)] = value.reshape(SUB * LANES)
    tile_copy = pltpu.make_async_copy(tile_buffer, tile_temp, tile_sem)
    tile_copy.start()
    for part in range(early, parts):
        solve_columns(part)
    tile_copy.wait()
    for part in range(parts):
        part_copy(part).wait()


def on_device(
    column_old,
    coupling,
    sea_temp,
    land_mask,
    tile_weight,
    tile_coeff,
    tile_capacity,
    tile_conduct,
    tile_old,
    tile_forcing,
):
    axes = ("lon", "lev")
    couplings, columns = coupling.shape
    levels = column_old.shape[0]
    tiles = tile_weight.shape[0]
    peers = lax.axis_size("lon")
    slot_count = columns // peers
    rows = columns // LANES
    blocks = rows // SUB
    fast = peers == SUB and rows == SUB * SUB
    devices = peers * lax.axis_size("lev")
    pairs = [(i, i ^ 1) for i in range(devices)]
    following = [(i, (i + 1 if i % 2 else i - 1) % devices) for i in range(devices)]
    hbm, vmem = pl.ANY, pltpu.VMEM
    full = (rows, LANES)
    mask = land_mask.reshape(full)
    table_outs = [
        VMEM(full, I32),
        VMEM(full, F32),
        VMEM(full, F32),
        VMEM((rows, 6 * rows), jnp.bfloat16),
        VMEM((2 * rows, 3 * rows), jnp.bfloat16),
        VMEM(full, I32),
    ]
    edge = (couplings, LANES)
    next_own, pair_own = chip_call(
        cut_edges,
        [VMEM(edge, F32)] * 2,
        [pltpu.HBM],
        [vmem] * 2,
        [DMA((2,))],
        (coupling,),
        pl.CostEstimate(flops=0, bytes_accessed=16 * couplings * LANES, transcendentals=0),
        EDGE_GRANT,
    )
    next_edge = lax.ppermute(next_own, axes, following)
    pair_edge = lax.ppermute(pair_own, axes, pairs)
    padded, source, first, second, place, fetch, spot = chip_call(
        functools.partial(prepare, fast),
        [VMEM((couplings, rows + 2 * SUB, LANES), F32)] + table_outs,
        [pltpu.HBM] * 2,
        [vmem] * 7,
        [VMEM(full, I32), DMA, DMA],
        (coupling, mask),
        pl.CostEstimate(
            flops=8 * couplings * columns, bytes_accessed=8 * levels * columns, transcendentals=0
        ),
        WIDE_GRANT,
    )
    sent = (peers, 6, SUB, LANES) if fast else (4,) + full
    handed = VMEM if fast else jax.ShapeDtypeStruct
    offset, factor, params, land, tile_base, tile_slope, send = chip_call(
        functools.partial(eliminate, fast),
        [
            VMEM((levels - 2,) + full, F32),
            VMEM((levels - 2,) + full, F32),
            VMEM((4,) + full, F32),
            handed((2,) + full, F32),
            VMEM((tiles,) + full, F32),
            VMEM((tiles,) + full, F32),
            handed(sent, F32),
        ],
        [vmem] * 8 + [pltpu.HBM] * 6,
        [vmem] * 7,
        [VMEM((couplings, LANES), F32)] * 2 + [VMEM((tiles, columns), F32)] * 6 + [DMA((6,))],
        (
            padded,
            on_chip(column_old),
            pair_edge,
            next_edge,
            source,
            first,
            second,
            place,
            tile_weight,
            tile_coeff,
            tile_capacity,
            tile_conduct,
            tile_old,
            tile_forcing,
        ),
        pl.CostEstimate(
            flops=20 * levels * columns, bytes_accessed=24 * tiles * columns, transcendentals=0
        ),
        TILE_GRANT,
    )
    if fast:
        inbox = lax.all_to_all(send, "lon", split_axis=0, concat_axis=0, tiled=True)
        slots = inbox
    else:
        ranked = send.reshape(4, slot_count, peers).transpose(2, 0, 1)
        own = land.reshape(2, peers, slot_count).transpose(1, 0, 2)
        got = lax.all_to_all(
            jnp.concatenate([own, ranked], axis=1), "lon", split_axis=0, concat_axis=0, tiled=True
        )
        inbox = got[:, :2].transpose(1, 2, 0).reshape((2,) + full)
        slots = got[:, 2:].transpose(1, 0, 2).reshape((4,) + full)
    width = 2
    column_temp, tile_temp = chip_call(
        functools.partial(finish, fast),
        [
            jax.ShapeDtypeStruct(column_old.shape, F32),
            jax.ShapeDtypeStruct(tile_old.shape, F32),
        ],
        [vmem] * 12,
        [hbm, hbm],
        [
            VMEM((2,) + full, F32),
            VMEM(full, F32),
            VMEM((2,) + full, F32),
            VMEM((levels, columns), F32),
            VMEM((tiles, columns), F32),
            DMA((blocks // width,)),
            DMA,
        ],
        (
            inbox,
            slots,
            offset,
            factor,
            params,
            land,
            tile_base,
            tile_slope,
            fetch,
            spot,
            mask,
            sea_temp.reshape(full),
        ),
        pl.CostEstimate(
            flops=4 * levels * columns, bytes_accessed=4 * levels * columns, transcendentals=0
        ),
    )
    return column_temp, tile_temp


def solution(mesh):
    wide, flat = P(None, ("lon", "lev")), P(("lon", "lev"))
    in_specs = (wide, wide, flat, flat) + (wide,) * 6
    return jax.shard_map(
        on_device, mesh=mesh, in_specs=in_specs, out_specs=(wide, wide), check_vma=False
    )
```
